128 devices in a mesh: heads: 2 (over z_hi), slab: 64 (over z_lo, y, x, core).
Axes of the slice: x: 4, y: 4, z: 4 (z_hi: 2, z_lo: 2; z = z_hi * 2 + z_lo), core: 2. Of those that a mesh axis runs over, the one named last changes fastest.
Arguments:
- tokens: bfloat16 [64, 384, 3072], P('slab', 'heads'), may hold values from -400 to 400
- qkv_weight: bfloat16 [3072, 4608], P(None, 'heads'), may hold values from -1 to 1
- out_weight: bfloat16 [1536, 3072], P('heads'), may hold values from -0.15625 to 0.15625
- query_gain: float32 [128], replicated, may hold values from 0.6 to 4.5
- key_gain: float32 [128], replicated, may hold values from 0.6 to 4.5
- mod_shift: float32 [3072], replicated, may hold values from -3 to 3
- mod_scale: float32 [3072], replicated, may hold values from -0.5 to 1.5
- branch_gate: float32 [3072], replicated, may hold values from 1 to 3
- block_mask: int32 [64, 27], P('slab'), may hold values 0 or 1
Outputs:
- attended: bfloat16 [64, 384, 3072], P('slab', 'heads')
The draws below stay inside these ranges and needn't reach their ends.
All inputs are finite; a program needn't handle non-finite values. No bound on the sum of `block_mask` on one device may be relied on, other than what follows from the above.
Results may differ from the reference program's by a relative error of at most 0.0095.
The reference program's roundings to bfloat16 on the way count: a program that leaves them out, or rounds other values in their place, can miss the bound.
Values may be sent and summed in bfloat16 or wider, within the bound.
No kernel may reach another device: no remote copies, remote signals or barrier semaphores. Data moves between devices by JAX's collectives and lax.ppermute only.
A program may use at most 320 MiB of HBM per device.

```python
import math
import jax
import jax.numpy as jnp
from jax import lax

D = 3072
ATT_HEADS = 12
HD = 128
TILE = 384
GT = 4
GH = 4
GW = 4
TILES = 64
N_HEADS = 2


def draw_tokens(key, part):
    key_base = jax.random.fold_in(key, 1)
    key_rows = jax.random.fold_in(key, 2)
    key_cols = jax.random.fold_in(key, 3)
    row_scale = jnp.exp(jax.random.uniform(key_rows, (TILES, TILE, 1), jnp.float32) * math.log(10.0))
    col_scale = jnp.exp(jax.random.uniform(key_cols, (D,), jnp.float32) * math.log(10.0))
    values_base = jnp.clip(jax.random.normal(key_base, (TILES, TILE, D), jnp.float32), -4.0, 4.0)
    return (values_base * row_scale * col_scale).astype(jnp.bfloat16)


def draw_qkv_weight(key, part):
    values_base = jnp.clip(jax.random.normal(jax.random.fold_in(key, 5), (D, ATT_HEADS, 3, HD), jnp.float32), -5.0, 5.0) * D ** (-0.5)
    return values_base.reshape(D, 3 * ATT_HEADS * HD).astype(jnp.bfloat16)


def draw_query_gain(key, part):
    return jax.random.uniform(jax.random.fold_in(key, 21), (HD,), jnp.float32, 0.6, 2.0)


def draw_key_gain(key, part):
    return jax.random.uniform(jax.random.fold_in(key, 31), (HD,), jnp.float32, 0.6, 2.0)


def plant(array, own_key, low, high):
    longest = array.shape.index(max(array.shape))
    spots = []
    for shift in (0, 1):
        where = [jax.random.randint(jax.random.fold_in(own_key, axis), (), 0, length) for axis, length in enumerate(array.shape)]
        where[longest] = (where[longest] + shift) % array.shape[longest]
        spots.append(tuple(where))
    return array.at[spots[0]].set(low).at[spots[1]].set(high)


def block_scale(stream_key, dims, cuts, low, largest):
    gain = 1.0
    for axis_at, blocks in cuts:
        draws = jax.random.uniform(jax.random.fold_in(jax.random.fold_in(stream_key, 6), axis_at), (blocks,), jnp.float32, low / len(cuts), largest / len(cuts))
        gain = gain * jnp.repeat(jnp.exp(draws), dims[axis_at] // blocks).reshape((-1,) + (1,) * (len(dims) - 1 - axis_at))
    return gain


def normal_values(stream_key, extent, spread, bound, cuts=(), kind=jnp.bfloat16):
    entries = spread * jax.random.normal(stream_key, extent, jnp.float32)
    if cuts:
        entries = entries * block_scale(stream_key, extent, cuts, -0.22, 0.18)
    return jnp.clip(entries, -bound, bound).astype(kind)


def setup_inputs(seed: int = 0) -> dict:
    seeds = jax.random.split(jax.random.key(seed), 10)
    return {
        "tokens": draw_tokens(jax.random.fold_in(seeds[9], 71), 0),
        "qkv_weight": draw_qkv_weight(jax.random.fold_in(seeds[9], 71), 0),
        "out_weight": normal_values(seeds[2], (ATT_HEADS * HD, D), (ATT_HEADS * HD) ** -0.5, 0.15625, ((0, 2),)),
        "query_gain": draw_query_gain(jax.random.fold_in(seeds[9], 71), 0),
        "key_gain": draw_key_gain(jax.random.fold_in(seeds[9], 71), 0),
        "mod_shift": normal_values(seeds[5], (D,), 0.5, 3.0, (), jnp.float32),
        "mod_scale": jnp.clip(jax.random.uniform(seeds[6], (D,), jnp.float32, -0.5, 1.5), -0.5, 1.5),
        "branch_gate": jnp.clip(jax.random.uniform(seeds[7], (D,), jnp.float32, 1.0, 3.0), 1.0, 3.0),
        "block_mask": plant((jax.random.randint(seeds[8], (TILES, 27), 0, 3) < 2).astype(jnp.int32), jax.random.fold_in(seeds[8], 1), 0, 1),
    }


def modulate(token_rows, mod_shift, mod_scale):
    token_rows = token_rows.astype(jnp.float32)
    row_mean = lax.optimization_barrier(jnp.mean(token_rows, axis=-1, keepdims=True))
    centered = token_rows - row_mean
    variance = lax.optimization_barrier(jnp.mean(centered * centered, axis=-1, keepdims=True))
    return (centered * lax.rsqrt(variance + 1e-06) * (1.0 + mod_scale) + mod_shift).astype(jnp.bfloat16)

def head_norm(head_rows, scale_gain):
    head_rows = head_rows.astype(jnp.float32)
    return head_rows * lax.rsqrt(lax.optimization_barrier(jnp.mean(head_rows * head_rows, axis=-1, keepdims=True)) + 1e-06) * scale_gain

def window_live(mask_row, slab_at, grid_t, grid_h, grid_w):
    time_at = slab_at // (grid_h * grid_w)
    height_at = slab_at // grid_w % grid_h
    width_at = slab_at % grid_w
    offsets = jnp.arange(27, dtype=jnp.int32)
    step_t = offsets // 9 - 1
    step_h = offsets // 3 % 3 - 1
    step_w = offsets % 3 - 1
    inside = (time_at + step_t >= 0) & (time_at + step_t < grid_t)
    inside = inside & (height_at + step_h >= 0) & (height_at + step_h < grid_h)
    inside = inside & (width_at + step_w >= 0) & (width_at + step_w < grid_w)
    return inside & ((offsets == 13) | (mask_row == 1))

def soft_weights(scores, live):
    keep = live[None, :, None]
    masked = jnp.where(keep, scores, -1e+30)
    row_top = lax.optimization_barrier(jnp.max(masked, axis=(1, 2), keepdims=True))
    raised = jnp.where(keep, jnp.exp(masked - row_top), 0.0)
    return (raised / lax.optimization_barrier(jnp.sum(raised, axis=(1, 2), keepdims=True))).astype(jnp.bfloat16)

def reference(tokens, qkv_weight, out_weight, query_gain, key_gain, mod_shift, mod_scale, branch_gate, block_mask):
    tile_count = tokens.shape[0]
    tile_tok = tokens.shape[1]
    normed = modulate(tokens, mod_shift, mod_scale)
    projected = jnp.dot(normed.reshape(-1, D), qkv_weight, preferred_element_type=jnp.float32).astype(jnp.bfloat16)
    pieces = projected.reshape(tile_count, tile_tok, ATT_HEADS, 3, HD)
    queries = (head_norm(pieces[:, :, :, 0], query_gain) * HD ** (-0.5)).astype(jnp.bfloat16)
    all_keys = head_norm(pieces[:, :, :, 1], key_gain).astype(jnp.bfloat16)
    all_values = pieces[:, :, :, 2]
    grid_shape = (GT, GH, GW, tile_tok, ATT_HEADS, HD)
    widths = ((1, 1), (1, 1), (1, 1), (0, 0), (0, 0), (0, 0))
    padded_keys = jnp.pad(all_keys.reshape(grid_shape), widths)
    padded_values = jnp.pad(all_values.reshape(grid_shape), widths)

    def one_tile(slab_at):
        time_at = slab_at // (GH * GW)
        height_at = slab_at // GW % GH
        width_at = slab_at % GW
        zero = jnp.zeros((), jnp.int32)
        starts = (time_at, height_at, width_at, zero, zero, zero)
        sizes = (3, 3, 3, tile_tok, ATT_HEADS, HD)
        window_keys = lax.dynamic_slice(padded_keys, starts, sizes).reshape(27, tile_tok, ATT_HEADS, HD)
        window_values = lax.dynamic_slice(padded_values, starts, sizes).reshape(27, tile_tok, ATT_HEADS, HD)
        own_queries = lax.dynamic_index_in_dim(queries, slab_at, 0, keepdims=False)
        mask_row = lax.dynamic_index_in_dim(block_mask, slab_at, 0, keepdims=False)
        live = window_live(mask_row, slab_at, GT, GH, GW)

        def one_head(head_at):
            query_rows = lax.dynamic_index_in_dim(own_queries, head_at, 1, keepdims=False).astype(jnp.float32)
            key_rows = lax.dynamic_index_in_dim(window_keys, head_at, 2, keepdims=False).astype(jnp.float32)
            value_rows = lax.dynamic_index_in_dim(window_values, head_at, 2, keepdims=False).astype(jnp.float32)
            scores = jnp.einsum('qd,okd->qok', query_rows, key_rows)
            weights = soft_weights(scores, live).astype(jnp.float32)
            return jnp.einsum('qok,okd->qd', weights, value_rows).astype(jnp.bfloat16)
        per_head = lax.map(one_head, jnp.arange(ATT_HEADS, dtype=jnp.int32))
        return jnp.transpose(per_head, (1, 0, 2))
    attention = lax.map(one_tile, jnp.arange(tile_count, dtype=jnp.int32))
    flat_rows = attention.reshape(tile_count * tile_tok, ATT_HEADS * HD)
    group_width = ATT_HEADS * HD // N_HEADS
    summed = jnp.zeros((tile_count * tile_tok, D), jnp.float32)
    for group_at in range(N_HEADS):
        lower = group_at * group_width
        term = jnp.dot(flat_rows[:, lower:lower + group_width], out_weight[lower:lower + group_width], preferred_element_type=jnp.float32)
        rounded = lax.optimization_barrier(term.astype(jnp.bfloat16))
        summed = summed + rounded.astype(jnp.float32)
    return (branch_gate * summed).astype(jnp.bfloat16).reshape(tile_count, tile_tok, D)
```

```python
import jax
import jax.numpy as jnp
import numpy as np
from jax import lax
from jax.experimental import pallas as pl
from jax.experimental.pallas import tpu as pltpu
from jax.sharding import PartitionSpec as P


TILE = 384
HD = 128
MASK_ROWS = 16
ROWS = TILE + MASK_ROWS
NEG = -1e30

HALO = (
    ((0, 0, 1), (0, 2, 4, 6)),
    ((0, 1, 0), (0, 1, 4, 5)),
    ((1, 0, 0), (0, 1, 2, 3)),
    ((0, 1, 1), (0, 4)),
    ((1, 0, 1), (0, 2)),
    ((1, 1, 0), (0, 1)),
    ((1, 1, 1), (0,)),
)
OWN_AT = [((u >> 2) & 1, (u >> 1) & 1, u & 1) for u in range(8)]
HALO_AT = [
    tuple(-1 if moved[d] else ((u >> (2 - d)) & 1) for d in range(3)) for moved, us in HALO for u in us
]


def chip_of(s):
    return ((s >> 4) & 1) * 2 + ((s >> 2) & 1)


def corner_of(s):
    return ((s >> 3) & 1) * 2 + ((s >> 1) & 1)


def slot_of(s, core, p):
    return chip_of(s) ^ p ^ (core * corner_of(s))


def u_base(s):
    ut = ((s >> 4) ^ (s >> 5) ^ 1) & 1
    uh = ((s >> 2) ^ (s >> 3) ^ 1) & 1
    uw = (s ^ (s >> 1) ^ 1) & 1
    return ut * 4 + uh * 2 + uw


def chip_mask(p):
    return ((p >> 1) << 4) | ((p & 1) << 2)


def halo_mask(core, moved):
    mask = (moved[0] << 5) | (moved[1] << 3) | (moved[2] << 1)
    if core:
        mask |= (moved[1] << 4) | (moved[2] << 2)
    return mask


def busy(s):
    return slot_of(s, s & 1, 0) < 3


def to_chip(value, p):
    pairs = [(s, s ^ chip_mask(p)) for s in range(64) if busy(s ^ chip_mask(p))]
    return lax.ppermute(value, "slab", pairs)


def from_chip(value, p):
    pairs = [(s, s ^ chip_mask(p)) for s in range(64) if busy(s)]
    return lax.ppermute(value, "slab", pairs)


def to_core(value):
    return lax.ppermute(value, "slab", [(s, s ^ 1) for s in range(64)])


def to_block(value, moved):
    pairs = [(s, s ^ halo_mask(s & 1, moved)) for s in range(64) if busy(s)]
    return lax.ppermute(value, "slab", pairs)


def to_group(value):
    return lax.ppermute(value, "heads", [(0, 1), (1, 0)])


def modulate(token_rows, mod_shift, mod_scale):
    token_rows = token_rows.astype(jnp.float32)
    row_mean = jnp.mean(token_rows, axis=-1, keepdims=True)
    centered = token_rows - row_mean
    variance = jnp.mean(centered * centered, axis=-1, keepdims=True)
    return (centered * lax.rsqrt(variance + 1e-06) * (1.0 + mod_scale) + mod_shift).astype(
        jnp.bfloat16
    )


def project_kernel(other, s_ref, own_ref, far_ref, w_ref, qg_ref, kg_ref, mask_ref, out_ref, x_ref):
    i = pl.program_id(0)
    half = own_ref.shape[0]

    @pl.when(i == 0)
    def _():
        x_ref[:half] = own_ref[...]
        x_ref[half:] = far_ref[...]

    s = s_ref[0]
    core = (s & 1) ^ other
    slot = slot_of(s, core, i)

    @pl.when(slot < 3)
    def _():
        acc = jnp.dot(x_ref[...], w_ref[...], preferred_element_type=jnp.float32).astype(jnp.bfloat16)

        def normed(part, gain):
            part = part.astype(jnp.float32)
            return part * lax.rsqrt(jnp.mean(part * part, axis=-1, keepdims=True) + 1e-06) * gain

        q = normed(acc[:, :HD], qg_ref[...]) * HD ** (-0.5)
        out_ref[0, :TILE, :HD] = q.astype(jnp.bfloat16)
        out_ref[0, :TILE, HD : 2 * HD] = normed(acc[:, HD : 2 * HD], kg_ref[...]).astype(jnp.bfloat16)
        out_ref[0, :TILE, 2 * HD :] = acc[:, 2 * HD :]
        out_ref[0, TILE:, :] = mask_ref[...]

    @pl.when(slot >= 3)
    def _():
        out_ref[0] = jnp.zeros_like(out_ref[0])


def project(slab_at, own, far, weight, query_gain, key_gain, mask_rows, other):
    half, width = own.shape

    def weight_at(i, s_ref):
        s = s_ref[0]
        core = (s & 1) ^ other
        return (0, core * 3 + jnp.minimum(slot_of(s, core, i), 2))

    full = lambda shape: pl.BlockSpec(shape, lambda i, s_ref: (0,) * len(shape))
    return pl.pallas_call(
        lambda *refs: project_kernel(other, *refs),
        out_shape=jax.ShapeDtypeStruct((4, ROWS, 3 * HD), jnp.bfloat16),
        grid_spec=pltpu.PrefetchScalarGridSpec(
            num_scalar_prefetch=1,
            grid=(4,),
            in_specs=[
                full((half, width)),
                full((half, width)),
                pl.BlockSpec((width, 3 * HD), weight_at),
                full((1, HD)),
                full((1, HD)),
                full((MASK_ROWS, 3 * HD)),
            ],
            out_specs=pl.BlockSpec((1, ROWS, 3 * HD), lambda i, s_ref: (i, 0, 0)),
            scratch_shapes=[pltpu.VMEM((2 * half, width), jnp.bfloat16)],
        ),
        name=f"project_{other}",
    )(slab_at, own, far, weight, query_gain, key_gain, mask_rows)


def assemble_kernel(s_ref, keep_ref, core_ref, a_ref, b_ref, c_ref, q_ref, kv_ref, mask_ref, *sends):
    base = u_base(s_ref[0])
    pieces = [(keep_ref, 0), (core_ref, 0)]
    for ref in (a_ref, b_ref, c_ref):
        pieces += [(ref, 0), (ref, 1)]
    for r, (ref, at) in enumerate(pieces):
        u = base ^ r
        q_ref[u] = ref[at, :TILE, :HD]
        kv_ref[u] = ref[at, :TILE, HD:]
        mask_ref[u] = ref[at, TILE : TILE + 8, :HD].astype(jnp.float32).astype(jnp.int32)
    for (_, us), send in zip(HALO, sends, strict=True):
        for at, u in enumerate(us):
            send[at] = kv_ref[u]


def assemble(slab_at, keep, core, near):
    whole = lambda shape: pl.BlockSpec(shape, lambda i, s_ref: (0,) * len(shape))
    shapes = [
        ((8, TILE, HD), jnp.bfloat16),
        ((8, TILE, 2 * HD), jnp.bfloat16),
        ((8, 8, HD), jnp.int32),
    ] + [((len(us), TILE, 2 * HD), jnp.bfloat16) for _, us in HALO]
    return pl.pallas_call(
        assemble_kernel,
        out_shape=[jax.ShapeDtypeStruct(*shape) for shape in shapes],
        grid_spec=pltpu.PrefetchScalarGridSpec(
            num_scalar_prefetch=1,
            grid=(1,),
            in_specs=[whole((1, ROWS, 3 * HD))] * 2 + [whole((2, ROWS, 3 * HD))] * 3,
            out_specs=[whole(shape) for shape, _ in shapes],
        ),
        name="assemble",
    )(slab_at, keep, core, *near)


def live_pair(s, u, at, mask_ref):
    signs = (((s >> 5) & 1) * 2 - 1, ((s >> 3) & 1) * 2 - 1, ((s >> 1) & 1) * 2 - 1)
    steps = [at[d] - ((u >> (2 - d)) & 1) for d in range(3)]
    inside = (steps[0] >= -1) & (steps[1] >= -1) & (steps[2] >= -1)
    offset = 13 + 9 * signs[0] * steps[0] + 3 * signs[1] * steps[1] + signs[2] * steps[2]
    offset = jnp.where(inside, offset, 13)
    return inside & ((offset == 13) | (mask_ref[u, offset] == 1))


def attend_tile(q, kv, m_ref, l_ref, acc_ref):
    scores = lax.dot_general(
        q, kv[:, :HD], (((1,), (1,)), ((), ())), preferred_element_type=jnp.float32
    )
    old = m_ref[...]
    top = jnp.maximum(old, jnp.max(scores, axis=1, keepdims=True))
    raised = jnp.exp(scores - top[:, :1])
    shrink = jnp.exp(old - top)
    m_ref[...] = top
    l_ref[...] = l_ref[...] * shrink + jnp.sum(raised, axis=1, keepdims=True)
    acc_ref[...] = acc_ref[...] * shrink + jnp.dot(
        raised.astype(jnp.bfloat16), kv[:, HD:], preferred_element_type=jnp.float32
    )


def own_kernel(s_ref, mask_ref, q_ref, kv_ref, m_ref, l_ref, acc_ref):
    s = s_ref[0]
    u = pl.program_id(0)
    m_ref[0] = jnp.full_like(m_ref[0], NEG)
    l_ref[0] = jnp.zeros_like(l_ref[0])
    acc_ref[0] = jnp.zeros_like(acc_ref[0])

    def step(k, _):
        at = ((k >> 2) & 1, (k >> 1) & 1, k & 1)

        @pl.when(live_pair(s, u, at, mask_ref))
        def _():
            attend_tile(q_ref[0], kv_ref[k], m_ref.at[0], l_ref.at[0], acc_ref.at[0])

        return 0

    lax.fori_loop(0, 8, step, 0)


def attend_own(slab_at, mask, q, kv):
    per_u = lambda shape: pl.BlockSpec((1, *shape), lambda u, *_: (u, 0, 0))
    state = jax.ShapeDtypeStruct((8, TILE, HD), jnp.float32)
    return pl.pallas_call(
        own_kernel,
        out_shape=[state, state, state],
        grid_spec=pltpu.PrefetchScalarGridSpec(
            num_scalar_prefetch=2,
            grid=(8,),
            in_specs=[
                per_u((TILE, HD)),
                pl.BlockSpec((8, TILE, 2 * HD), lambda u, *_: (0, 0, 0)),
            ],
            out_specs=[per_u((TILE, HD))] * 3,
        ),
        name="attend_own",
    )(slab_at, mask, q, kv)


def halo_kernel(s_ref, mask_ref, at_ref, q_ref, m_in, l_in, acc_in, kv_ref, out_ref, m_ref, l_ref, acc_ref):
    s = s_ref[0]
    u = pl.program_id(0) ^ u_base(s)
    m_ref[...] = m_in[0]
    l_ref[...] = l_in[0]
    acc_ref[...] = acc_in[0]

    def step(k, _):
        at = tuple(at_ref[3 * k + d] for d in range(3))

        @pl.when(live_pair(s, u, at, mask_ref))
        def _():
            attend_tile(q_ref[0], kv_ref[k], m_ref, l_ref, acc_ref)

        return 0

    lax.fori_loop(0, len(HALO_AT), step, 0)
    out_ref[0] = (acc_ref[...] / l_ref[...]).astype(jnp.bfloat16)


def attend_halo(slab_at, mask, q, state, kv):
    table = jnp.asarray(np.array(HALO_AT, np.int32).reshape(-1))
    per_u = pl.BlockSpec((1, TILE, HD), lambda r, s_ref, *_: (r ^ u_base(s_ref[0]), 0, 0))
    return pl.pallas_call(
        halo_kernel,
        out_shape=jax.ShapeDtypeStruct((8, TILE, HD), jnp.bfloat16),
        grid_spec=pltpu.PrefetchScalarGridSpec(
            num_scalar_prefetch=3,
            grid=(8,),
            in_specs=[per_u] * 4 + [pl.BlockSpec(kv.shape, lambda r, *_: (0, 0, 0))],
            out_specs=pl.BlockSpec((1, TILE, HD), lambda r, *_: (r, 0, 0)),
            scratch_shapes=[pltpu.VMEM((TILE, HD), jnp.float32)] * 3,
        ),
        name="attend_halo",
    )(slab_at, mask, table, q, *state, kv)


def output_kernel(s_ref, own_ref, a_ref, b_ref, c_ref, core_ref, w_ref, out_ref, x_ref):
    s = s_ref[0]

    @pl.when(pl.program_id(0) == 0)
    def _():
        for p, ref in enumerate((own_ref, a_ref, b_ref, c_ref)):
            for core, piece in ((s & 1, ref.at[0]), (1 - (s & 1), core_ref.at[p])):
                slot = slot_of(s, core, p)

                @pl.when(slot < 3)
                def _(core=core, slot=slot, piece=piece):
                    head = core * 3 + slot
                    x_ref[:, pl.ds(pl.multiple_of(head * HD, HD), HD)] = piece[...]

    out_ref[...] = jnp.dot(
        x_ref[...], w_ref[...], preferred_element_type=jnp.float32
    ).astype(jnp.bfloat16)


def output(slab_at, own, near, core, weight, half_at):
    inner, width = weight.shape
    half = TILE // 2
    cols = 1024
    one = pl.BlockSpec((1, half, HD), lambda n, s_ref: (0, half_at, 0))
    return pl.pallas_call(
        output_kernel,
        out_shape=jax.ShapeDtypeStruct((half, width), jnp.bfloat16),
        grid_spec=pltpu.PrefetchScalarGridSpec(
            num_scalar_prefetch=1,
            grid=(width // cols,),
            in_specs=[one] * 4
            + [
                pl.BlockSpec((4, half, HD), lambda n, s_ref: (0, half_at, 0)),
                pl.BlockSpec((inner, cols), lambda n, s_ref: (0, n)),
            ],
            out_specs=pl.BlockSpec((half, cols), lambda n, s_ref: (0, n)),
            scratch_shapes=[pltpu.VMEM((half, inner), jnp.bfloat16)],
        ),
        name=f"output_{half_at}",
    )(slab_at, own, *near, core, weight)


def on_device(
    tokens,
    qkv_weight,
    out_weight,
    query_gain,
    key_gain,
    mod_shift,
    mod_scale,
    branch_gate,
    block_mask,
):
    slab_at = lax.axis_index("slab").astype(jnp.int32).reshape(1)
    own = modulate(tokens[0], mod_shift, mod_scale)
    far = to_group(own)
    mask_rows = jnp.pad(
        jnp.broadcast_to(block_mask.astype(jnp.bfloat16), (MASK_ROWS, 27)), ((0, 0), (0, 3 * HD - 27))
    )
    gains = (query_gain.reshape(1, HD), key_gain.reshape(1, HD))
    send = project(slab_at, own, far, qkv_weight, *gains, mask_rows, 1)
    core = to_core(send)
    keep = project(slab_at, own, far, qkv_weight, *gains, mask_rows, 0)
    near = [to_chip(jnp.stack([keep[p], core[p]]), p) for p in (1, 2, 3)]
    q, kv, mask, *sends = assemble(slab_at, keep, core, near)
    mask = mask[:, 0, :]
    halo = [to_block(piece, moved) for piece, (moved, _) in zip(sends, HALO, strict=True)]
    state = attend_own(slab_at, mask, q, kv)
    mixed = attend_halo(slab_at, mask, q, state, jnp.concatenate(halo, axis=0))
    back = [from_chip(mixed[2 * p : 2 * p + 2], p) for p in (1, 2, 3)]
    crossed = to_core(jnp.stack([mixed[1]] + [piece[1] for piece in back]))
    far_partial = output(slab_at, mixed, back, crossed, out_weight, 1)
    received = to_group(far_partial)
    own_partial = output(slab_at, mixed, back, crossed, out_weight, 0)
    summed = own_partial.astype(jnp.float32) + received.astype(jnp.float32)
    return (branch_gate * summed).astype(jnp.bfloat16)[None]


def solution(mesh):
    in_specs = (
        P("slab", "heads", None),
        P(None, "heads"),
        P("heads", None),
        P(),
        P(),
        P(),
        P(),
        P(),
        P("slab", None),
    )
    out_specs = P("slab", "heads", None)
    return jax.shard_map(
        on_device, mesh=mesh, in_specs=in_specs, out_specs=out_specs, check_vma=False
    )
```

```python
import jax
import jax.numpy as jnp
import numpy as np
from jax import lax
from jax.experimental import pallas as pl
from jax.experimental.pallas import tpu as pltpu
from jax.sharding import PartitionSpec as P


TILE = 384
HD = 128
MASK_ROWS = 16
NEG = -1e30

HALO = (
    ((0, 0, 1), (0, 2, 4, 6)),
    ((0, 1, 0), (0, 1, 4, 5)),
    ((1, 0, 0), (0, 1, 2, 3)),
    ((0, 1, 1), (0, 4)),
    ((1, 0, 1), (0, 2)),
    ((1, 1, 0), (0, 1)),
    ((1, 1, 1), (0,)),
)
OWN_AT = [((u >> 2) & 1, (u >> 1) & 1, u & 1) for u in range(8)]
HALO_AT = [
    tuple(-1 if moved[d] else ((u >> (2 - d)) & 1) for d in range(3)) for moved, us in HALO for u in us
]


def chip_of(s):
    return ((s >> 4) & 1) * 2 + ((s >> 2) & 1)


def corner_of(s):
    return ((s >> 3) & 1) * 2 + ((s >> 1) & 1)


def slot_of(s, core, p):
    return chip_of(s) ^ p ^ (core * corner_of(s))


def u_base(s):
    ut = ((s >> 4) ^ (s >> 5) ^ 1) & 1
    uh = ((s >> 2) ^ (s >> 3) ^ 1) & 1
    uw = (s ^ (s >> 1) ^ 1) & 1
    return ut * 4 + uh * 2 + uw


def chip_mask(p):
    return ((p >> 1) << 4) | ((p & 1) << 2)


def halo_mask(core, moved):
    mask = (moved[0] << 5) | (moved[1] << 3) | (moved[2] << 1)
    if core:
        mask |= (moved[1] << 4) | (moved[2] << 2)
    return mask


def busy(s):
    return slot_of(s, s & 1, 0) < 3


def to_chip(value, p):
    pairs = [(s, s ^ chip_mask(p)) for s in range(64) if busy(s ^ chip_mask(p))]
    return lax.ppermute(value, "slab", pairs)


def from_chip(value, p):
    pairs = [(s, s ^ chip_mask(p)) for s in range(64) if busy(s)]
    return lax.ppermute(value, "slab", pairs)


def across(value):
    pairs = [(64 * g + s, 64 * (1 - g) + s) for g in range(2) for s in range(64) if busy(s)]
    return lax.ppermute(value, ("heads", "slab"), pairs)


def weight_across(value):
    pairs = [(64 * g + s, 64 * (1 - g) + (s ^ 32)) for g in range(2) for s in range(64)]
    return lax.ppermute(value, ("heads", "slab"), pairs)


def to_core(value):
    return lax.ppermute(value, "slab", [(s, s ^ 1) for s in range(64)])


def to_block(value, moved):
    pairs = [(s, s ^ halo_mask(s & 1, moved)) for s in range(64) if busy(s)]
    return lax.ppermute(value, "slab", pairs)


def to_group(value):
    return lax.ppermute(value, "heads", [(0, 1), (1, 0)])


def whole(shape):
    return pl.BlockSpec(shape, lambda *_: (0,) * len(shape), pipeline_mode=pl.Buffered(1))


def modulate(token_rows, mod_shift, mod_scale):
    token_rows = token_rows.astype(jnp.float32)
    row_mean = jnp.mean(token_rows, axis=-1, keepdims=True)
    centered = token_rows - row_mean
    variance = jnp.mean(centered * centered, axis=-1, keepdims=True)
    return (centered * lax.rsqrt(variance + 1e-06) * (1.0 + mod_scale) + mod_shift).astype(
        jnp.bfloat16
    )


def project_kernel(other, s_ref, x_ref, w_ref, qg_ref, kg_ref, mask_ref, out_ref):
    s = s_ref[0]
    rows = x_ref.shape[0]
    slot = slot_of(s, (s & 1) ^ other, pl.program_id(0))

    @pl.when(slot < 3)
    def _():
        acc = jnp.dot(x_ref[...], w_ref[...], preferred_element_type=jnp.float32).astype(jnp.bfloat16)

        def normed(part, gain):
            part = part.astype(jnp.float32)
            return part * lax.rsqrt(jnp.mean(part * part, axis=-1, keepdims=True) + 1e-06) * gain

        q = normed(acc[:, :HD], qg_ref[...]) * HD ** (-0.5)
        out_ref[0, :rows, :HD] = q.astype(jnp.bfloat16)
        out_ref[0, :rows, HD : 2 * HD] = normed(acc[:, HD : 2 * HD], kg_ref[...]).astype(jnp.bfloat16)
        out_ref[0, :rows, 2 * HD :] = acc[:, 2 * HD :]
        if out_ref.shape[1] > rows:
            out_ref[0, rows:, :] = mask_ref[...]

    @pl.when(slot >= 3)
    def _():
        out_ref[0] = jnp.zeros_like(out_ref[0])


def project(slab_at, x, weight, query_gain, key_gain, mask_rows, other, with_mask):
    rows, width = x.shape
    out_rows = rows + (MASK_ROWS if with_mask else 0)

    def weight_at(i, s_ref):
        s = s_ref[0]
        core = (s & 1) ^ other
        return (0, core * 3 + jnp.minimum(slot_of(s, core, i), 2))

    return pl.pallas_call(
        lambda *refs: project_kernel(other, *refs),
        out_shape=jax.ShapeDtypeStruct((4, out_rows, 3 * HD), jnp.bfloat16),
        grid_spec=pltpu.PrefetchScalarGridSpec(
            num_scalar_prefetch=1,
            grid=(4,),
            in_specs=[
                whole((rows, width)),
                pl.BlockSpec((width, 3 * HD), weight_at),
                whole((1, HD)),
                whole((1, HD)),
                whole((MASK_ROWS, 3 * HD)),
            ],
            out_specs=pl.BlockSpec((1, out_rows, 3 * HD), lambda i, s_ref: (i, 0, 0)),
        ),
        compiler_params=pltpu.CompilerParams(vmem_limit_bytes=7 << 20),
    )(slab_at, x, weight, query_gain, key_gain, mask_rows)


def live_tables():
    table = np.full((8, 8, HD), HD, np.int32)
    for corner in range(8):
        signs = [((corner >> (2 - d)) & 1) * 2 - 1 for d in range(3)]
        for u in range(8):
            for k, at in enumerate(OWN_AT + HALO_AT):
                steps = [at[d] - ((u >> (2 - d)) & 1) for d in range(3)]
                if min(steps) >= -1:
                    table[corner, u, k] = 13 + sum(
                        w * g * t for w, g, t in zip((9, 3, 1), signs, steps, strict=True)
                    )
    return table


def block_of(s):
    return ((s >> 5) & 1) * 4 + corner_of(s)


def part_kernel(s_ref, w_ref, out_ref, sem):
    rows = out_ref.shape[0]
    start = pl.multiple_of((s_ref[0] & 1) * rows, rows)
    copy = pltpu.make_async_copy(w_ref.at[pl.ds(start, rows)], out_ref, sem)
    copy.start()
    copy.wait()


def weight_part(slab_at, weight):
    rows, width = weight.shape
    return pl.pallas_call(
        part_kernel,
        out_shape=jax.ShapeDtypeStruct((rows // 2, width), weight.dtype),
        grid_spec=pltpu.PrefetchScalarGridSpec(
            num_scalar_prefetch=1,
            grid=(1,),
            in_specs=[pl.BlockSpec(memory_space=pl.ANY)],
            out_specs=pl.BlockSpec(memory_space=pl.ANY),
            scratch_shapes=[pltpu.SemaphoreType.DMA(())],
        ),
        compiler_params=pltpu.CompilerParams(vmem_limit_bytes=1 << 20),
        name="weight_part",
    )(slab_at, weight)


def assemble_kernel(s_ref, *refs):
    base = u_base(s_ref[0])
    half = TILE // 2
    spot_ref, q_ref, kv_ref, live_ref = refs[10:14]
    entry = lax.broadcasted_iota(jnp.int32, (HD, HD), 0)
    lane = lax.broadcasted_iota(jnp.int32, (MASK_ROWS, HD), 1)
    for at, halves in enumerate((refs[:5], refs[5:10])):
        keep_ref, core_ref, *near = halves
        pieces = [(keep_ref, 0), (core_ref, 0)] + [(ref, dc) for ref in near for dc in range(2)]
        rows = slice(at * half, (at + 1) * half)
        for r, (ref, dc) in enumerate(pieces):
            u = base ^ r
            q_ref[u, rows] = ref[dc, :half, :HD]
            kv_ref[u, rows] = ref[dc, :half, HD:]
            if at == 0:
                marked = jnp.where(lane == 13, 1.0, ref[dc, half:, :HD].astype(jnp.float32))
                pick = jnp.where(entry == spot_ref[0, pl.ds(u, 1)], 1.0, 0.0)
                live = jnp.dot(
                    marked.astype(jnp.bfloat16),
                    pick.astype(jnp.bfloat16),
                    preferred_element_type=jnp.float32,
                )
                live_ref[pl.ds(u, 1)] = live[:1].astype(jnp.int32)
    for (_, us), send in zip(HALO, refs[14:]):
        for at, u in enumerate(us):
            send[at] = kv_ref[u]


def assemble(slab_at, halves):
    shapes = [
        ((8, TILE, HD), jnp.bfloat16),
        ((8, TILE, 2 * HD), jnp.bfloat16),
        ((8, HD), jnp.int32),
    ] + [((len(us), TILE, 2 * HD), jnp.bfloat16) for _, us in HALO[:4]]
    in_specs = []
    for keep, *_ in halves:
        rows = keep.shape[1]
        in_specs += [whole((1, rows, 3 * HD))] * 2 + [whole((2, rows, 3 * HD))] * 3
    in_specs.append(pl.BlockSpec((1, 8, HD), lambda i, s_ref: (block_of(s_ref[0]), 0, 0)))
    return pl.pallas_call(
        assemble_kernel,
        out_shape=[jax.ShapeDtypeStruct(*shape) for shape in shapes],
        grid_spec=pltpu.PrefetchScalarGridSpec(
            num_scalar_prefetch=1,
            grid=(1,),
            in_specs=in_specs,
            out_specs=[whole(shape) for shape, _ in shapes],
        ),
        compiler_params=pltpu.CompilerParams(vmem_limit_bytes=16 << 20),
        name="assemble",
    )(slab_at, *halves[0], *halves[1], jnp.asarray(live_tables()))


def fold(x, op):
    return op(op(x[:, :HD], x[:, HD : 2 * HD]), x[:, 2 * HD :])


def spread_max(x):
    return jnp.broadcast_to(jnp.max(x, axis=1, keepdims=True), x.shape)


def attend(u, first, count, live_ref, q, kv_ref, s_ref, list_ref, m_ref, l_ref, acc_ref, rescale):
    n = jnp.int32(0)
    for k in range(count):
        list_ref[n] = k
        n = n + live_ref[u, first + k]

    def score(base, group):
        def step(j, _):
            top = m_ref[...]
            for i in range(group):
                at = base + j * group + i
                scores = lax.dot_general(
                    q,
                    kv_ref[list_ref[at], :, :HD],
                    (((1,), (1,)), ((), ())),
                    preferred_element_type=jnp.float32,
                )
                s_ref[at] = scores
                top = jnp.maximum(top, fold(scores, jnp.maximum))
            m_ref[...] = top
            return 0

        return step

    def weigh(base, group):
        def step(j, _):
            top = m_ref[...]
            top = jnp.concatenate([top, top, top], axis=1)
            total = l_ref[...]
            acc = acc_ref[...]
            for i in range(group):
                at = base + j * group + i
                raised = jnp.exp(s_ref[at] - top)
                total = total + fold(raised, jnp.add)
                acc = acc + jnp.dot(
                    raised.astype(jnp.bfloat16),
                    kv_ref[list_ref[at], :, HD:],
                    preferred_element_type=jnp.float32,
                )
            l_ref[...] = total
            acc_ref[...] = acc
            return 0

        return step

    def each(make):
        lax.fori_loop(0, n >> 2, make(0, 4), 0)
        lax.fori_loop(0, (n >> 1) & 1, make((n >> 2) << 2, 2), 0)
        lax.fori_loop(0, n & 1, make((n >> 1) << 1, 1), 0)

    each(score)
    rescale(spread_max(m_ref[...]))
    each(weigh)


def own_kernel(live_ref, q_ref, kv_ref, m_ref, l_ref, acc_ref, s_ref, list_ref):
    u = pl.program_id(0)
    m, l, acc = m_ref.at[0], l_ref.at[0], acc_ref.at[0]
    m[...] = jnp.full_like(m[...], NEG)

    def rescale(top):
        m[...] = top
        l[...] = jnp.zeros_like(l[...])
        acc[...] = jnp.zeros_like(acc[...])

    attend(u, 0, 8, live_ref, q_ref[0], kv_ref, s_ref, list_ref, m, l, acc, rescale)


def attend_own(live, q, kv):
    per_u = pl.BlockSpec((1, TILE, HD), lambda u, *_: (u, 0, 0))
    state = jax.ShapeDtypeStruct((8, TILE, HD), jnp.float32)
    return pl.pallas_call(
        own_kernel,
        out_shape=[state, state, state],
        grid_spec=pltpu.PrefetchScalarGridSpec(
            num_scalar_prefetch=1,
            grid=(8,),
            in_specs=[per_u, whole((8, TILE, 2 * HD))],
            out_specs=[per_u] * 3,
            scratch_shapes=[pltpu.VMEM((8, TILE, TILE), jnp.float32), pltpu.SMEM((9,), jnp.int32)],
        ),
        compiler_params=pltpu.CompilerParams(vmem_limit_bytes=14 << 20),
        name="attend_own",
    )(live, q, kv)


def halo_kernel(s_ref, live_ref, q_ref, m_in, l_in, acc_in, *refs):
    pieces, (near_ref, far_ref, kv_ref, score_ref, m_ref, l_ref, acc_ref, list_ref, sems) = refs[:7], refs[7:]

    @pl.when(pl.program_id(0) == 0)
    def _():
        at = 0
        copies = []
        for i, piece in enumerate(pieces):
            to = kv_ref.at[pl.ds(at, piece.shape[0])]
            copies.append(pltpu.make_async_copy(piece, to, sems.at[i]))
            at += piece.shape[0]
        for copy in copies:
            copy.start()
        for copy in copies:
            copy.wait()

    u = pl.program_id(0) ^ u_base(s_ref[0])
    m_ref[...] = m_in[0]

    def rescale(top):
        m_ref[...] = top
        shrink = jnp.exp(m_in[0] - top)
        l_ref[...] = l_in[0] * shrink
        acc_ref[...] = acc_in[0] * shrink

    count = len(HALO_AT)
    attend(u, 8, count, live_ref, q_ref[0], kv_ref, score_ref, list_ref, m_ref, l_ref, acc_ref, rescale)
    total = jnp.sum(l_ref[...], axis=1, keepdims=True)
    mixed = (acc_ref[...] / total).astype(jnp.bfloat16)
    near_ref[0] = mixed[: TILE // 2]
    far_ref[0] = mixed[TILE // 2 :]


def attend_halo(slab_at, live, q, state, pieces):
    per_u = pl.BlockSpec((1, TILE, HD), lambda r, s_ref, *_: (r ^ u_base(s_ref[0]), 0, 0))
    count = len(HALO_AT)
    return pl.pallas_call(
        halo_kernel,
        out_shape=[jax.ShapeDtypeStruct((8, TILE // 2, HD), jnp.bfloat16)] * 2,
        grid_spec=pltpu.PrefetchScalarGridSpec(
            num_scalar_prefetch=2,
            grid=(8,),
            in_specs=[per_u] * 4 + [pl.BlockSpec(memory_space=pl.ANY)] * len(pieces),
            out_specs=[pl.BlockSpec((1, TILE // 2, HD), lambda r, *_: (r, 0, 0))] * 2,
            scratch_shapes=[
                pltpu.VMEM((count, TILE, 2 * HD), jnp.bfloat16),
                pltpu.VMEM((count, TILE, TILE), jnp.float32),
            ]
            + [pltpu.VMEM((TILE, HD), jnp.float32)] * 3
            + [pltpu.SMEM((count + 1,), jnp.int32), pltpu.SemaphoreType.DMA((len(pieces),))],
        ),
        compiler_params=pltpu.CompilerParams(vmem_limit_bytes=24 << 20),
        name="attend_halo",
    )(slab_at, live, q, *state, *pieces)


def output_kernel(s_ref, *refs):
    same, cross, (core_ref, w_ref, wc_ref, wd_ref, gate_ref, out_ref, x_ref, xc_ref, xd_ref) = (
        refs[:4],
        refs[4:8],
        refs[8:],
    )
    s = s_ref[0]
    mine = s & 1

    @pl.when(pl.program_id(0) == 0)
    def _():
        for p in range(4):
            for core, pieces in (
                (mine, (same[p].at[0], cross[p].at[0])),
                (1 - mine, (core_ref.at[p], core_ref.at[4 + p])),
            ):
                slot = slot_of(s, core, p)
                far_ref = xc_ref if core is mine else xd_ref

                @pl.when(slot < 3)
                def _(core=core, slot=slot, pieces=pieces, far_ref=far_ref):
                    x_ref[:, pl.ds(pl.multiple_of((core * 3 + slot) * HD, HD), HD)] = pieces[0][...]
                    far_ref[:, pl.ds(pl.multiple_of(slot * HD, HD), HD)] = pieces[1][...]

    def dot(x, w):
        return jnp.dot(x[...], w[...], preferred_element_type=jnp.float32)

    near = dot(x_ref, w_ref).astype(jnp.bfloat16).astype(jnp.float32)
    far = (dot(xc_ref, wc_ref) + dot(xd_ref, wd_ref)).astype(jnp.bfloat16).astype(jnp.float32)
    out_ref[...] = (gate_ref[...] * (near + far)).astype(jnp.bfloat16)


def output(slab_at, same, cross, core, weight, weight_c, weight_d, gate):
    inner, width = weight.shape
    half = TILE // 2
    cols = 1024
    by_col = lambda rows: pl.BlockSpec((rows, cols), lambda n, s_ref: (0, n))
    return pl.pallas_call(
        output_kernel,
        out_shape=jax.ShapeDtypeStruct((half, width), jnp.bfloat16),
        grid_spec=pltpu.PrefetchScalarGridSpec(
            num_scalar_prefetch=1,
            grid=(width // cols,),
            in_specs=[whole((1, half, HD))] * 8
            + [whole((8, half, HD)), by_col(inner), by_col(inner // 2), by_col(inner // 2), by_col(1)],
            out_specs=by_col(half),
            scratch_shapes=[
                pltpu.VMEM((half, inner), jnp.bfloat16),
                pltpu.VMEM((half, inner // 2), jnp.bfloat16),
                pltpu.VMEM((half, inner // 2), jnp.bfloat16),
            ],
        ),
        compiler_params=pltpu.CompilerParams(vmem_limit_bytes=14 << 20),
        name="output",
    )(slab_at, *same, *cross, core, weight, weight_c, weight_d, gate)


def on_device(
    tokens,
    qkv_weight,
    out_weight,
    query_gain,
    key_gain,
    mod_shift,
    mod_scale,
    branch_gate,
    block_mask,
):
    slab_at = lax.axis_index("slab").astype(jnp.int32).reshape(1)
    own = modulate(tokens[0], mod_shift, mod_scale)
    far = to_group(own)
    mask_rows = jnp.pad(
        jnp.broadcast_to(block_mask.astype(jnp.bfloat16), (MASK_ROWS, 27)), ((0, 0), (0, 3 * HD - 27))
    )
    gains = (query_gain.reshape(1, HD), key_gain.reshape(1, HD))
    part = weight_part(slab_at, out_weight)
    halves = []
    x = own
    for at in range(2):
        send = project(slab_at, x, qkv_weight, *gains, mask_rows, 1, at == 0)
        if at:
            send, part = lax.optimization_barrier((send, part))
        core = to_core(send)
        keep = project(slab_at, x, qkv_weight, *gains, mask_rows, 0, at == 0)
        near = []
        for p in (1, 2, 3):
            near.append(to_chip(jnp.stack([keep[p], core[p]]), p))
        x = far
        halves.append((keep, core, *near))
    weight_c = weight_across(part)
    q, kv, live, *sends = assemble(slab_at, halves)
    halo = [to_block(piece, moved) for piece, (moved, _) in zip(sends, HALO)] + [None] * 3
    state = attend_own(live, q, kv)
    *state, over, weight_c = lax.optimization_barrier((*state, halo[2], weight_c))
    halo[2] = over
    for at, moved, us in ((4, (0, 0, 1), (0, 2)), (5, (0, 1, 0), (0, 1)), (6, (0, 1, 1), (0,))):
        halo[at] = to_block(jnp.stack([over[u] for u in us]), moved)
    weight_d = to_core(weight_c)
    mixed, crossing = attend_halo(slab_at, live, q, state, halo)
    crossed = across(crossing)
    pieces = [(mixed, crossed)]
    for p in (1, 2, 3):
        r = slice(2 * p, 2 * p + 2)
        moved = from_chip(jnp.concatenate([mixed[r], crossed[r]]), p)
        pieces.append((moved[:2], moved[2:]))
    same, cross = zip(*pieces, strict=True)
    core = to_core(jnp.stack([piece[1] for piece in same + cross]))
    gate = branch_gate.reshape(1, -1)
    return output(slab_at, same, cross, core, out_weight, weight_c, weight_d, gate)[None]


def solution(mesh):
    in_specs = (
        P("slab", "heads", None),
        P(None, "heads"),
        P("heads", None),
        P(),
        P(),
        P(),
        P(),
        P(),
        P("slab", None),
    )
    out_specs = P("slab", "heads", None)
    return jax.shard_map(
        on_device,
        mesh=mesh,
        in_specs=in_specs,
        out_specs=out_specs,
        check_vma=False,
    )
```

```python
import jax
import jax.numpy as jnp
import numpy as np
from jax import lax
from jax.experimental import pallas as pl
from jax.experimental.pallas import tpu as pltpu
from jax.sharding import PartitionSpec as P


TILE = 384
HD = 128
MASK_ROWS = 16
NEG = -1e30

HALO = (
    ((0, 0, 1), (0, 2, 4, 6)),
    ((0, 1, 0), (0, 1, 4, 5)),
    ((1, 0, 0), (0, 1, 2, 3)),
    ((0, 1, 1), (0, 4)),
    ((1, 0, 1), (0, 2)),
    ((1, 1, 0), (0, 1)),
    ((1, 1, 1), (0,)),
)
OWN_AT = [((u >> 2) & 1, (u >> 1) & 1, u & 1) for u in range(8)]
HALO_AT = [
    tuple(-1 if moved[d] else ((u >> (2 - d)) & 1) for d in range(3)) for moved, us in HALO for u in us
]


def chip_of(s):
    return ((s >> 4) & 1) * 2 + ((s >> 2) & 1)


def corner_of(s):
    return ((s >> 3) & 1) * 2 + ((s >> 1) & 1)


def slot_of(s, core, p):
    return chip_of(s) ^ p ^ (core * corner_of(s))


def u_base(s):
    ut = ((s >> 4) ^ (s >> 5) ^ 1) & 1
    uh = ((s >> 2) ^ (s >> 3) ^ 1) & 1
    uw = (s ^ (s >> 1) ^ 1) & 1
    return ut * 4 + uh * 2 + uw


def chip_mask(p):
    return ((p >> 1) << 4) | ((p & 1) << 2)


def halo_mask(core, moved):
    mask = (moved[0] << 5) | (moved[1] << 3) | (moved[2] << 1)
    if core:
        mask |= (moved[1] << 4) | (moved[2] << 2)
    return mask


def busy(s):
    return slot_of(s, s & 1, 0) < 3


def to_chip(value, p):
    pairs = [(s, s ^ chip_mask(p)) for s in range(64) if busy(s ^ chip_mask(p))]
    return lax.ppermute(value, "slab", pairs)


def from_chip(value, p):
    pairs = [(s, s ^ chip_mask(p)) for s in range(64) if busy(s)]
    return lax.ppermute(value, "slab", pairs)


def across(value):
    pairs = [(64 * g + s, 64 * (1 - g) + s) for g in range(2) for s in range(64) if busy(s)]
    return lax.ppermute(value, ("heads", "slab"), pairs)


def weight_across(value):
    pairs = [(64 * g + s, 64 * (1 - g) + (s ^ 32)) for g in range(2) for s in range(64)]
    return lax.ppermute(value, ("heads", "slab"), pairs)


def to_core(value):
    return lax.ppermute(value, "slab", [(s, s ^ 1) for s in range(64)])


def to_block(value, moved):
    pairs = [(s, s ^ halo_mask(s & 1, moved)) for s in range(64) if busy(s)]
    return lax.ppermute(value, "slab", pairs)


def to_group(value):
    return lax.ppermute(value, "heads", [(0, 1), (1, 0)])


def whole(shape):
    return pl.BlockSpec(shape, lambda *_: (0,) * len(shape), pipeline_mode=pl.Buffered(1))


def modulate_kernel(x_ref, shift_ref, scale_ref, out_ref):
    rows = x_ref[0].astype(jnp.float32)
    centered = rows - jnp.mean(rows, axis=-1, keepdims=True)
    variance = jnp.mean(centered * centered, axis=-1, keepdims=True)
    out = centered * lax.rsqrt(variance + 1e-06) * (1.0 + scale_ref[...]) + shift_ref[...]
    out_ref[...] = out.astype(jnp.bfloat16)


def modulate(tokens, mod_shift, mod_scale):
    _, rows, width = tokens.shape
    step = 48
    return pl.pallas_call(
        modulate_kernel,
        out_shape=jax.ShapeDtypeStruct((rows, width), jnp.bfloat16),
        grid=(rows // step,),
        in_specs=[
            pl.BlockSpec((1, step, width), lambda i: (0, i, 0)),
            whole((1, width)),
            whole((1, width)),
        ],
        out_specs=pl.BlockSpec((step, width), lambda i: (i, 0)),
        compiler_params=pltpu.CompilerParams(vmem_limit_bytes=8 << 20),
        name="modulate",
    )(tokens, mod_shift.reshape(1, width), mod_scale.reshape(1, width))


def project_kernel(other, s_ref, x_ref, w_ref, qg_ref, kg_ref, mask_ref, out_ref):
    s = s_ref[0]
    rows = x_ref.shape[0]
    slot = slot_of(s, (s & 1) ^ other, pl.program_id(0))

    @pl.when(slot < 3)
    def _():
        acc = jnp.dot(x_ref[...], w_ref[...], preferred_element_type=jnp.float32).astype(jnp.bfloat16)

        def normed(part, gain):
            part = part.astype(jnp.float32)
            return part * lax.rsqrt(jnp.mean(part * part, axis=-1, keepdims=True) + 1e-06) * gain

        q = normed(acc[:, :HD], qg_ref[...]) * HD ** (-0.5)
        out_ref[0, :rows, :HD] = q.astype(jnp.bfloat16)
        out_ref[0, :rows, HD : 2 * HD] = normed(acc[:, HD : 2 * HD], kg_ref[...]).astype(jnp.bfloat16)
        out_ref[0, :rows, 2 * HD :] = acc[:, 2 * HD :]
        if out_ref.shape[1] > rows:
            out_ref[0, rows:, :] = mask_ref[...]

    @pl.when(slot >= 3)
    def _():
        out_ref[0] = jnp.zeros_like(out_ref[0])


def project(slab_at, x, weight, query_gain, key_gain, mask_rows, other, with_mask):
    rows, width = x.shape
    out_rows = rows + (MASK_ROWS if with_mask else 0)

    def weight_at(i, s_ref):
        s = s_ref[0]
        core = (s & 1) ^ other
        return (0, core * 3 + jnp.minimum(slot_of(s, core, i), 2))

    return pl.pallas_call(
        lambda *refs: project_kernel(other, *refs),
        out_shape=jax.ShapeDtypeStruct((4, out_rows, 3 * HD), jnp.bfloat16),
        grid_spec=pltpu.PrefetchScalarGridSpec(
            num_scalar_prefetch=1,
            grid=(4,),
            in_specs=[
                whole((rows, width)),
                pl.BlockSpec((width, 3 * HD), weight_at),
                whole((1, HD)),
                whole((1, HD)),
                whole((MASK_ROWS, 3 * HD)),
            ],
            out_specs=pl.BlockSpec((1, out_rows, 3 * HD), lambda i, s_ref: (i, 0, 0)),
        ),
        compiler_params=pltpu.CompilerParams(vmem_limit_bytes=7 << 20),
    )(slab_at, x, weight, query_gain, key_gain, mask_rows)


def live_tables():
    table = np.full((8, 8, HD), HD, np.int32)
    for corner in range(8):
        signs = [((corner >> (2 - d)) & 1) * 2 - 1 for d in range(3)]
        for u in range(8):
            for k, at in enumerate(OWN_AT + HALO_AT):
                steps = [at[d] - ((u >> (2 - d)) & 1) for d in range(3)]
                if min(steps) >= -1:
                    table[corner, u, k] = 13 + sum(
                        w * g * t for w, g, t in zip((9, 3, 1), signs, steps, strict=True)
                    )
    return table


def block_of(s):
    return ((s >> 5) & 1) * 4 + corner_of(s)


def part_kernel(s_ref, w_ref, out_ref, sem):
    rows = out_ref.shape[0]
    start = pl.multiple_of((s_ref[0] & 1) * rows, rows)
    copy = pltpu.make_async_copy(w_ref.at[pl.ds(start, rows)], out_ref, sem)
    copy.start()
    copy.wait()


def weight_part(slab_at, weight):
    rows, width = weight.shape
    return pl.pallas_call(
        part_kernel,
        out_shape=jax.ShapeDtypeStruct((rows // 2, width), weight.dtype),
        grid_spec=pltpu.PrefetchScalarGridSpec(
            num_scalar_prefetch=1,
            grid=(1,),
            in_specs=[pl.BlockSpec(memory_space=pl.ANY)],
            out_specs=pl.BlockSpec(memory_space=pl.ANY),
            scratch_shapes=[pltpu.SemaphoreType.DMA(())],
        ),
        compiler_params=pltpu.CompilerParams(vmem_limit_bytes=1 << 20),
        name="weight_part",
    )(slab_at, weight)


def assemble_kernel(s_ref, *refs):
    base = u_base(s_ref[0])
    half = TILE // 2
    spot_ref, q_ref, kv_ref, live_ref = refs[10:14]
    entry = lax.broadcasted_iota(jnp.int32, (HD, HD), 0)
    lane = lax.broadcasted_iota(jnp.int32, (MASK_ROWS, HD), 1)
    for at, halves in enumerate((refs[:5], refs[5:10])):
        keep_ref, core_ref, *near = halves
        pieces = [(keep_ref, 0), (core_ref, 0)] + [(ref, dc) for ref in near for dc in range(2)]
        rows = slice(at * half, (at + 1) * half)
        for r, (ref, dc) in enumerate(pieces):
            u = base ^ r
            q_ref[u, rows] = ref[dc, :half, :HD]
            kv_ref[u, rows] = ref[dc, :half, HD:]
            if at == 0:
                marked = jnp.where(lane == 13, 1.0, ref[dc, half:, :HD].astype(jnp.float32))
                pick = jnp.where(entry == spot_ref[0, pl.ds(u, 1)], 1.0, 0.0)
                live = jnp.dot(
                    marked.astype(jnp.bfloat16),
                    pick.astype(jnp.bfloat16),
                    preferred_element_type=jnp.float32,
                )
                live_ref[pl.ds(u, 1)] = live[:1].astype(jnp.int32)
    for (_, us), send in zip(HALO, refs[14:]):
        for at, u in enumerate(us):
            send[at] = kv_ref[u]


def assemble(slab_at, halves):
    shapes = [
        ((8, TILE, HD), jnp.bfloat16),
        ((8, TILE, 2 * HD), jnp.bfloat16),
        ((8, HD), jnp.int32),
    ] + [((len(us), TILE, 2 * HD), jnp.bfloat16) for _, us in HALO[:4]]
    in_specs = []
    for keep, *_ in halves:
        rows = keep.shape[1]
        in_specs += [whole((1, rows, 3 * HD))] * 2 + [whole((2, rows, 3 * HD))] * 3
    in_specs.append(pl.BlockSpec((1, 8, HD), lambda i, s_ref: (block_of(s_ref[0]), 0, 0)))
    return pl.pallas_call(
        assemble_kernel,
        out_shape=[jax.ShapeDtypeStruct(*shape) for shape in shapes],
        grid_spec=pltpu.PrefetchScalarGridSpec(
            num_scalar_prefetch=1,
            grid=(1,),
            in_specs=in_specs,
            out_specs=[whole(shape) for shape, _ in shapes],
        ),
        compiler_params=pltpu.CompilerParams(vmem_limit_bytes=16 << 20),
        name="assemble",
    )(slab_at, *halves[0], *halves[1], jnp.asarray(live_tables()))


def fold(x, op):
    return op(op(x[:, :HD], x[:, HD : 2 * HD]), x[:, 2 * HD :])


def spread_max(x):
    return jnp.broadcast_to(jnp.max(x, axis=1, keepdims=True), x.shape)


def attend(u, first, count, live_ref, q, kv_ref, s_ref, list_ref, m_ref, l_ref, acc_ref, rescale):
    n = jnp.int32(0)
    for k in range(count):
        list_ref[n] = k
        n = n + live_ref[u, first + k]

    def score(base, group):
        def step(j, _):
            top = m_ref[...]
            for i in range(group):
                at = base + j * group + i
                scores = lax.dot_general(
                    q,
                    kv_ref[list_ref[at], :, :HD],
                    (((1,), (1,)), ((), ())),
                    preferred_element_type=jnp.float32,
                )
                s_ref[at] = scores
                top = jnp.maximum(top, fold(scores, jnp.maximum))
            m_ref[...] = top
            return 0

        return step

    def weigh(base, group):
        def step(j, _):
            top = m_ref[...]
            top = jnp.concatenate([top, top, top], axis=1)
            total = l_ref[...]
            acc = acc_ref[...]
            for i in range(group):
                at = base + j * group + i
                raised = jnp.exp(s_ref[at] - top)
                total = total + fold(raised, jnp.add)
                acc = acc + jnp.dot(
                    raised.astype(jnp.bfloat16),
                    kv_ref[list_ref[at], :, HD:],
                    preferred_element_type=jnp.float32,
                )
            l_ref[...] = total
            acc_ref[...] = acc
            return 0

        return step

    def each(make):
        lax.fori_loop(0, n >> 2, make(0, 4), 0)
        lax.fori_loop(0, (n >> 1) & 1, make((n >> 2) << 2, 2), 0)
        lax.fori_loop(0, n & 1, make((n >> 1) << 1, 1), 0)

    each(score)
    rescale(spread_max(m_ref[...]))
    each(weigh)


def own_kernel(live_ref, q_ref, kv_ref, m_ref, l_ref, acc_ref, s_ref, list_ref):
    u = pl.program_id(0)
    m, l, acc = m_ref.at[0], l_ref.at[0], acc_ref.at[0]
    m[...] = jnp.full_like(m[...], NEG)

    def rescale(top):
        m[...] = top
        l[...] = jnp.zeros_like(l[...])
        acc[...] = jnp.zeros_like(acc[...])

    attend(u, 0, 8, live_ref, q_ref[0], kv_ref, s_ref, list_ref, m, l, acc, rescale)


def attend_own(live, q, kv):
    per_u = pl.BlockSpec((1, TILE, HD), lambda u, *_: (u, 0, 0))
    state = jax.ShapeDtypeStruct((8, TILE, HD), jnp.float32)
    return pl.pallas_call(
        own_kernel,
        out_shape=[state, state, state],
        grid_spec=pltpu.PrefetchScalarGridSpec(
            num_scalar_prefetch=1,
            grid=(8,),
            in_specs=[per_u, whole((8, TILE, 2 * HD))],
            out_specs=[per_u] * 3,
            scratch_shapes=[pltpu.VMEM((8, TILE, TILE), jnp.float32), pltpu.SMEM((9,), jnp.int32)],
        ),
        compiler_params=pltpu.CompilerParams(vmem_limit_bytes=14 << 20),
        name="attend_own",
    )(live, q, kv)


def halo_kernel(first, s_ref, live_ref, q_ref, m_in, l_in, acc_in, *refs):
    pieces, (near_ref, far_ref, kv_ref, score_ref, m_ref, l_ref, acc_ref, list_ref, sems) = refs[:7], refs[7:]

    @pl.when(pl.program_id(0) == 0)
    def _():
        at = 0
        copies = []
        for i, piece in enumerate(pieces):
            to = kv_ref.at[pl.ds(at, piece.shape[0])]
            copies.append(pltpu.make_async_copy(piece, to, sems.at[i]))
            at += piece.shape[0]
        for copy in copies:
            copy.start()
        for copy in copies:
            copy.wait()

    u = (first + pl.program_id(0)) ^ u_base(s_ref[0])
    m_ref[...] = m_in[0]

    def rescale(top):
        m_ref[...] = top
        shrink = jnp.exp(m_in[0] - top)
        l_ref[...] = l_in[0] * shrink
        acc_ref[...] = acc_in[0] * shrink

    count = len(HALO_AT)
    attend(u, 8, count, live_ref, q_ref[0], kv_ref, score_ref, list_ref, m_ref, l_ref, acc_ref, rescale)
    total = jnp.sum(l_ref[...], axis=1, keepdims=True)
    mixed = (acc_ref[...] / total).astype(jnp.bfloat16)
    near_ref[0] = mixed[: TILE // 2]
    far_ref[0] = mixed[TILE // 2 :]


def attend_halo(slab_at, live, q, state, pieces, first):
    per_u = pl.BlockSpec((1, TILE, HD), lambda r, s_ref, *_: ((first + r) ^ u_base(s_ref[0]), 0, 0))
    count = len(HALO_AT)
    return pl.pallas_call(
        lambda *refs: halo_kernel(first, *refs),
        out_shape=[jax.ShapeDtypeStruct((4, TILE // 2, HD), jnp.bfloat16)] * 2,
        grid_spec=pltpu.PrefetchScalarGridSpec(
            num_scalar_prefetch=2,
            grid=(4,),
            in_specs=[per_u] * 4 + [pl.BlockSpec(memory_space=pl.ANY)] * len(pieces),
            out_specs=[pl.BlockSpec((1, TILE // 2, HD), lambda r, *_: (r, 0, 0))] * 2,
            scratch_shapes=[
                pltpu.VMEM((count, TILE, 2 * HD), jnp.bfloat16),
                pltpu.VMEM((count, TILE, TILE), jnp.float32),
            ]
            + [pltpu.VMEM((TILE, HD), jnp.float32)] * 3
            + [pltpu.SMEM((count + 1,), jnp.int32), pltpu.SemaphoreType.DMA((len(pieces),))],
        ),
        compiler_params=pltpu.CompilerParams(vmem_limit_bytes=24 << 20),
    )(slab_at, live, q, *state, *pieces)


def output_kernel(s_ref, *refs):
    same, cross, (core_ref, w_ref, wc_ref, wd_ref, gate_ref, out_ref, x_ref, xc_ref, xd_ref) = (
        refs[:4],
        refs[4:8],
        refs[8:],
    )
    s = s_ref[0]
    mine = s & 1

    @pl.when(pl.program_id(0) == 0)
    def _():
        for p in range(4):
            for core, pieces in (
                (mine, (same[p].at[0], cross[p].at[0])),
                (1 - mine, (core_ref.at[p], core_ref.at[4 + p])),
            ):
                slot = slot_of(s, core, p)
                far_ref = xc_ref if core is mine else xd_ref

                @pl.when(slot < 3)
                def _(core=core, slot=slot, pieces=pieces, far_ref=far_ref):
                    x_ref[:, pl.ds(pl.multiple_of((core * 3 + slot) * HD, HD), HD)] = pieces[0][...]
                    far_ref[:, pl.ds(pl.multiple_of(slot * HD, HD), HD)] = pieces[1][...]

    def dot(x, w):
        return jnp.dot(x[...], w[...], preferred_element_type=jnp.float32)

    near = dot(x_ref, w_ref).astype(jnp.bfloat16).astype(jnp.float32)
    far = (dot(xc_ref, wc_ref) + dot(xd_ref, wd_ref)).astype(jnp.bfloat16).astype(jnp.float32)
    out_ref[...] = (gate_ref[...] * (near + far)).astype(jnp.bfloat16)


def output(slab_at, same, cross, core, weight, weight_c, weight_d, gate):
    inner, width = weight.shape
    half = TILE // 2
    cols = 1024
    by_col = lambda rows: pl.BlockSpec((rows, cols), lambda n, s_ref: (0, n))
    return pl.pallas_call(
        output_kernel,
        out_shape=jax.ShapeDtypeStruct((half, width), jnp.bfloat16),
        grid_spec=pltpu.PrefetchScalarGridSpec(
            num_scalar_prefetch=1,
            grid=(width // cols,),
            in_specs=[whole((1, half, HD))] * 8
            + [whole((8, half, HD)), by_col(inner), by_col(inner // 2), by_col(inner // 2), by_col(1)],
            out_specs=by_col(half),
            scratch_shapes=[
                pltpu.VMEM((half, inner), jnp.bfloat16),
                pltpu.VMEM((half, inner // 2), jnp.bfloat16),
                pltpu.VMEM((half, inner // 2), jnp.bfloat16),
            ],
        ),
        compiler_params=pltpu.CompilerParams(vmem_limit_bytes=14 << 20),
        name="output",
    )(slab_at, *same, *cross, core, weight, weight_c, weight_d, gate)


def on_device(
    tokens,
    qkv_weight,
    out_weight,
    query_gain,
    key_gain,
    mod_shift,
    mod_scale,
    branch_gate,
    block_mask,
):
    slab_at = lax.axis_index("slab").astype(jnp.int32).reshape(1)
    own = modulate(tokens, mod_shift, mod_scale)
    far = to_group(own)
    mask_rows = jnp.pad(
        jnp.broadcast_to(block_mask.astype(jnp.bfloat16), (MASK_ROWS, 27)), ((0, 0), (0, 3 * HD - 27))
    )
    gains = (query_gain.reshape(1, HD), key_gain.reshape(1, HD))
    part = weight_part(slab_at, out_weight)
    halves = []
    x = own
    for at in range(2):
        send = project(slab_at, x, qkv_weight, *gains, mask_rows, 1, at == 0)
        if at:
            send, part = lax.optimization_barrier((send, part))
        core = to_core(send)
        keep = project(slab_at, x, qkv_weight, *gains, mask_rows, 0, at == 0)
        near = []
        for p in (1, 2, 3):
            near.append(to_chip(jnp.stack([keep[p], core[p]]), p))
        x = far
        halves.append((keep, core, *near))
    weight_c = weight_across(part)
    q, kv, live, *sends = assemble(slab_at, halves)
    halo = [to_block(piece, moved) for piece, (moved, _) in zip(sends, HALO)] + [None] * 3
    state = attend_own(live, q, kv)
    *state, over = lax.optimization_barrier((*state, halo[2]))
    halo[2] = over
    for at, moved, us in ((4, (0, 0, 1), (0, 2)), (5, (0, 1, 0), (0, 1)), (6, (0, 1, 1), (0,))):
        halo[at] = to_block(jnp.stack([over[u] for u in us]), moved)
    done = {}
    for first in (4, 0):
        mixed, crossing = attend_halo(slab_at, live, q, state, halo, first)
        if not first:
            mixed, weight_c = lax.optimization_barrier((mixed, weight_c))
        crossed = across(crossing)
        for p in (first // 2, first // 2 + 1):
            r = slice(2 * p - first, 2 * p - first + 2)
            done[p] = (mixed[r], crossed[r])
    weight_d = to_core(weight_c)
    for p in (2, 3, 1):
        moved = from_chip(jnp.concatenate(done[p]), p)
        done[p] = (moved[:2], moved[2:])
    same, cross = zip(*(done[p] for p in range(4)), strict=True)
    core = to_core(jnp.stack([piece[1] for piece in same + cross]))
    gate = branch_gate.reshape(1, -1)
    return output(slab_at, same, cross, core, out_weight, weight_c, weight_d, gate)[None]


def solution(mesh):
    in_specs = (
        P("slab", "heads", None),
        P(None, "heads"),
        P("heads", None),
        P(),
        P(),
        P(),
        P(),
        P(),
        P("slab", None),
    )
    out_specs = P("slab", "heads", None)
    return jax.shard_map(
        on_device,
        mesh=mesh,
        in_specs=in_specs,
        out_specs=out_specs,
        check_vma=False,
    )
```

```python
import jax
import jax.numpy as jnp
import numpy as np
from jax import lax
from jax.experimental import pallas as pl
from jax.experimental.pallas import tpu as pltpu
from jax.sharding import PartitionSpec as P


TILE = 384
HD = 128
MASK_ROWS = 16
NEG = -1e30

HALO = (
    ((0, 0, 1), (0, 2, 4, 6)),
    ((0, 1, 0), (0, 1, 4, 5)),
    ((1, 0, 0), (0, 1, 2, 3)),
    ((0, 1, 1), (0, 4)),
    ((1, 0, 1), (0, 2)),
    ((1, 1, 0), (0, 1)),
    ((1, 1, 1), (0,)),
)
OWN_AT = [((u >> 2) & 1, (u >> 1) & 1, u & 1) for u in range(8)]
HALO_AT = [
    tuple(-1 if moved[d] else ((u >> (2 - d)) & 1) for d in range(3)) for moved, us in HALO for u in us
]


def chip_of(s):
    return ((s >> 4) & 1) * 2 + ((s >> 2) & 1)


def corner_of(s):
    return ((s >> 3) & 1) * 2 + ((s >> 1) & 1)


def slot_of(s, core, p):
    return chip_of(s) ^ p ^ (core * corner_of(s))


def u_base(s):
    ut = ((s >> 4) ^ (s >> 5) ^ 1) & 1
    uh = ((s >> 2) ^ (s >> 3) ^ 1) & 1
    uw = (s ^ (s >> 1) ^ 1) & 1
    return ut * 4 + uh * 2 + uw


def chip_mask(p):
    return ((p >> 1) << 4) | ((p & 1) << 2)


def halo_mask(core, moved):
    mask = (moved[0] << 5) | (moved[1] << 3) | (moved[2] << 1)
    if core:
        mask |= (moved[1] << 4) | (moved[2] << 2)
    return mask


def busy(s):
    return slot_of(s, s & 1, 0) < 3


def to_chip(value, p):
    pairs = [(s, s ^ chip_mask(p)) for s in range(64) if busy(s ^ chip_mask(p))]
    return lax.ppermute(value, "slab", pairs)


def from_chip(value, p):
    pairs = [(s, s ^ chip_mask(p)) for s in range(64) if busy(s)]
    return lax.ppermute(value, "slab", pairs)


def across(value):
    pairs = [(64 * g + s, 64 * (1 - g) + s) for g in range(2) for s in range(64) if busy(s)]
    return lax.ppermute(value, ("heads", "slab"), pairs)


def weight_across(value):
    pairs = [(64 * g + s, 64 * (1 - g) + (s ^ 32)) for g in range(2) for s in range(64)]
    return lax.ppermute(value, ("heads", "slab"), pairs)


def to_core(value):
    return lax.ppermute(value, "slab", [(s, s ^ 1) for s in range(64)])


def to_block(value, moved):
    pairs = [(s, s ^ halo_mask(s & 1, moved)) for s in range(64) if busy(s)]
    return lax.ppermute(value, "slab", pairs)


def to_group(value):
    return lax.ppermute(value, "heads", [(0, 1), (1, 0)])


def whole(shape):
    return pl.BlockSpec(shape, lambda *_: (0,) * len(shape), pipeline_mode=pl.Buffered(1))


def modulate_kernel(x_ref, shift_ref, scale_ref, out_ref):
    rows = x_ref[0].astype(jnp.float32)
    centered = rows - jnp.mean(rows, axis=-1, keepdims=True)
    variance = jnp.mean(centered * centered, axis=-1, keepdims=True)
    out = centered * lax.rsqrt(variance + 1e-06) * (1.0 + scale_ref[...]) + shift_ref[...]
    out_ref[...] = out.astype(jnp.bfloat16)


def modulate(tokens, mod_shift, mod_scale):
    _, rows, width = tokens.shape
    step = 48
    return pl.pallas_call(
        modulate_kernel,
        out_shape=jax.ShapeDtypeStruct((rows, width), jnp.bfloat16),
        grid=(rows // step,),
        in_specs=[
            pl.BlockSpec((1, step, width), lambda i: (0, i, 0)),
            whole((1, width)),
            whole((1, width)),
        ],
        out_specs=pl.BlockSpec((step, width), lambda i: (i, 0)),
        compiler_params=pltpu.CompilerParams(vmem_limit_bytes=8 << 20),
        name="modulate",
    )(tokens, mod_shift.reshape(1, width), mod_scale.reshape(1, width))


def project_kernel(other, s_ref, x_ref, w_ref, qg_ref, kg_ref, mask_ref, out_ref):
    s = s_ref[0]
    rows = x_ref.shape[0]
    slot = slot_of(s, (s & 1) ^ other, pl.program_id(0))

    @pl.when(slot < 3)
    def _():
        acc = jnp.dot(x_ref[...], w_ref[...], preferred_element_type=jnp.float32).astype(jnp.bfloat16)

        def normed(part, gain):
            part = part.astype(jnp.float32)
            return part * lax.rsqrt(jnp.mean(part * part, axis=-1, keepdims=True) + 1e-06) * gain

        q = normed(acc[:, :HD], qg_ref[...]) * HD ** (-0.5)
        out_ref[0, :rows, :HD] = q.astype(jnp.bfloat16)
        out_ref[0, :rows, HD : 2 * HD] = normed(acc[:, HD : 2 * HD], kg_ref[...]).astype(jnp.bfloat16)
        out_ref[0, :rows, 2 * HD :] = acc[:, 2 * HD :]
        if out_ref.shape[1] > rows:
            out_ref[0, rows:, :] = mask_ref[...]

    @pl.when(slot >= 3)
    def _():
        out_ref[0] = jnp.zeros_like(out_ref[0])


def project(slab_at, x, weight, query_gain, key_gain, mask_rows, other, with_mask):
    rows, width = x.shape
    out_rows = rows + (MASK_ROWS if with_mask else 0)

    def weight_at(i, s_ref):
        s = s_ref[0]
        core = (s & 1) ^ other
        return (0, core * 3 + jnp.minimum(slot_of(s, core, i), 2))

    return pl.pallas_call(
        lambda *refs: project_kernel(other, *refs),
        out_shape=jax.ShapeDtypeStruct((4, out_rows, 3 * HD), jnp.bfloat16),
        grid_spec=pltpu.PrefetchScalarGridSpec(
            num_scalar_prefetch=1,
            grid=(4,),
            in_specs=[
                whole((rows, width)),
                pl.BlockSpec((width, 3 * HD), weight_at),
                whole((1, HD)),
                whole((1, HD)),
                whole((MASK_ROWS, 3 * HD)),
            ],
            out_specs=pl.BlockSpec((1, out_rows, 3 * HD), lambda i, s_ref: (i, 0, 0)),
        ),
        compiler_params=pltpu.CompilerParams(vmem_limit_bytes=7 << 20),
    )(slab_at, x, weight, query_gain, key_gain, mask_rows)


def live_tables():
    table = np.full((8, 8, HD), HD, np.int32)
    for corner in range(8):
        signs = [((corner >> (2 - d)) & 1) * 2 - 1 for d in range(3)]
        for u in range(8):
            for k, at in enumerate(OWN_AT + HALO_AT):
                steps = [at[d] - ((u >> (2 - d)) & 1) for d in range(3)]
                if min(steps) >= -1:
                    table[corner, u, k] = 13 + sum(
                        w * g * t for w, g, t in zip((9, 3, 1), signs, steps, strict=True)
                    )
    return table


def block_of(s):
    return ((s >> 5) & 1) * 4 + corner_of(s)


def part_kernel(s_ref, w_ref, out_ref, sem):
    rows = out_ref.shape[0]
    start = pl.multiple_of((s_ref[0] & 1) * rows, rows)
    copy = pltpu.make_async_copy(w_ref.at[pl.ds(start, rows)], out_ref, sem)
    copy.start()
    copy.wait()


def weight_part(slab_at, weight):
    rows, width = weight.shape
    return pl.pallas_call(
        part_kernel,
        out_shape=jax.ShapeDtypeStruct((rows // 2, width), weight.dtype),
        grid_spec=pltpu.PrefetchScalarGridSpec(
            num_scalar_prefetch=1,
            grid=(1,),
            in_specs=[pl.BlockSpec(memory_space=pl.ANY)],
            out_specs=pl.BlockSpec(memory_space=pl.ANY),
            scratch_shapes=[pltpu.SemaphoreType.DMA(())],
        ),
        compiler_params=pltpu.CompilerParams(vmem_limit_bytes=1 << 20),
        name="weight_part",
    )(slab_at, weight)


def assemble_kernel(s_ref, *refs):
    base = u_base(s_ref[0])
    half = TILE // 2
    spot_ref, q_ref, kv_ref, live_ref = refs[10:14]
    entry = lax.broadcasted_iota(jnp.int32, (HD, HD), 0)
    lane = lax.broadcasted_iota(jnp.int32, (MASK_ROWS, HD), 1)
    for at, halves in enumerate((refs[:5], refs[5:10])):
        keep_ref, core_ref, *near = halves
        pieces = [(keep_ref, 0), (core_ref, 0)] + [(ref, dc) for ref in near for dc in range(2)]
        rows = slice(at * half, (at + 1) * half)
        for r, (ref, dc) in enumerate(pieces):
            u = base ^ r
            q_ref[u, rows] = ref[dc, :half, :HD]
            kv_ref[u, rows] = ref[dc, :half, HD:]
            if at == 0:
                marked = jnp.where(lane == 13, 1.0, ref[dc, half:, :HD].astype(jnp.float32))
                pick = jnp.where(entry == spot_ref[0, pl.ds(u, 1)], 1.0, 0.0)
                live = jnp.dot(
                    marked.astype(jnp.bfloat16),
                    pick.astype(jnp.bfloat16),
                    preferred_element_type=jnp.float32,
                )
                live_ref[pl.ds(u, 1)] = live[:1].astype(jnp.int32)
    for (_, us), send in zip(HALO, refs[14:]):
        for at, u in enumerate(us):
            send[at] = kv_ref[u]


def assemble(slab_at, halves):
    shapes = [
        ((8, TILE, HD), jnp.bfloat16),
        ((8, TILE, 2 * HD), jnp.bfloat16),
        ((8, HD), jnp.int32),
    ] + [((len(us), TILE, 2 * HD), jnp.bfloat16) for _, us in HALO[:4]]
    in_specs = []
    for keep, *_ in halves:
        rows = keep.shape[1]
        in_specs += [whole((1, rows, 3 * HD))] * 2 + [whole((2, rows, 3 * HD))] * 3
    in_specs.append(pl.BlockSpec((1, 8, HD), lambda i, s_ref: (block_of(s_ref[0]), 0, 0)))
    return pl.pallas_call(
        assemble_kernel,
        out_shape=[jax.ShapeDtypeStruct(*shape) for shape in shapes],
        grid_spec=pltpu.PrefetchScalarGridSpec(
            num_scalar_prefetch=1,
            grid=(1,),
            in_specs=in_specs,
            out_specs=[whole(shape) for shape, _ in shapes],
        ),
        compiler_params=pltpu.CompilerParams(vmem_limit_bytes=16 << 20),
        name="assemble",
    )(slab_at, *halves[0], *halves[1], jnp.asarray(live_tables()))


def fold(x, op):
    return op(op(x[:, :HD], x[:, HD : 2 * HD]), x[:, 2 * HD :])


def spread_max(x):
    return jnp.broadcast_to(jnp.max(x, axis=1, keepdims=True), x.shape)


def attend(u, first, count, live_ref, q, kv_ref, s_ref, list_ref, m_ref, l_ref, acc_ref, rescale):
    n = jnp.int32(0)
    for k in range(count):
        list_ref[n] = k
        n = n + live_ref[u, first + k]

    def score(base, group):
        def step(j, _):
            top = m_ref[...]
            for i in range(group):
                at = base + j * group + i
                scores = lax.dot_general(
                    q,
                    kv_ref[list_ref[at], :, :HD],
                    (((1,), (1,)), ((), ())),
                    preferred_element_type=jnp.float32,
                )
                s_ref[at] = scores
                top = jnp.maximum(top, fold(scores, jnp.maximum))
            m_ref[...] = top
            return 0

        return step

    def weigh(base, group):
        def step(j, _):
            top = m_ref[...]
            top = jnp.concatenate([top, top, top], axis=1)
            total = l_ref[...]
            acc = acc_ref[...]
            for i in range(group):
                at = base + j * group + i
                raised = jnp.exp(s_ref[at] - top)
                total = total + fold(raised, jnp.add)
                acc = acc + jnp.dot(
                    raised.astype(jnp.bfloat16),
                    kv_ref[list_ref[at], :, HD:],
                    preferred_element_type=jnp.float32,
                )
            l_ref[...] = total
            acc_ref[...] = acc
            return 0

        return step

    def each(make):
        lax.fori_loop(0, n >> 2, make(0, 4), 0)
        lax.fori_loop(0, (n >> 1) & 1, make((n >> 2) << 2, 2), 0)
        lax.fori_loop(0, n & 1, make((n >> 1) << 1, 1), 0)

    each(score)
    rescale(spread_max(m_ref[...]))
    each(weigh)


def own_kernel(live_ref, q_ref, kv_ref, m_ref, l_ref, acc_ref, s_ref, list_ref):
    u = pl.program_id(0)
    m, l, acc = m_ref.at[0], l_ref.at[0], acc_ref.at[0]
    m[...] = jnp.full_like(m[...], NEG)

    def rescale(top):
        m[...] = top
        l[...] = jnp.zeros_like(l[...])
        acc[...] = jnp.zeros_like(acc[...])

    attend(u, 0, 8, live_ref, q_ref[0], kv_ref, s_ref, list_ref, m, l, acc, rescale)


def attend_own(live, q, kv):
    per_u = pl.BlockSpec((1, TILE, HD), lambda u, *_: (u, 0, 0))
    state = jax.ShapeDtypeStruct((8, TILE, HD), jnp.float32)
    return pl.pallas_call(
        own_kernel,
        out_shape=[state, state, state],
        grid_spec=pltpu.PrefetchScalarGridSpec(
            num_scalar_prefetch=1,
            grid=(8,),
            in_specs=[per_u, whole((8, TILE, 2 * HD))],
            out_specs=[per_u] * 3,
            scratch_shapes=[pltpu.VMEM((8, TILE, TILE), jnp.float32), pltpu.SMEM((9,), jnp.int32)],
        ),
        compiler_params=pltpu.CompilerParams(vmem_limit_bytes=14 << 20),
        name="attend_own",
    )(live, q, kv)


def halo_kernel(first, s_ref, live_ref, q_ref, m_in, l_in, acc_in, *refs):
    pieces, (near_ref, far_ref, kv_ref, score_ref, m_ref, l_ref, acc_ref, list_ref, sems) = refs[:7], refs[7:]

    @pl.when(pl.program_id(0) == 0)
    def _():
        at = 0
        copies = []
        for i, piece in enumerate(pieces):
            to = kv_ref.at[pl.ds(at, piece.shape[0])]
            copies.append(pltpu.make_async_copy(piece, to, sems.at[i]))
            at += piece.shape[0]
        for copy in copies:
            copy.start()
        for copy in copies:
            copy.wait()

    u = (first + pl.program_id(0)) ^ u_base(s_ref[0])
    m_ref[...] = m_in[0]

    def rescale(top):
        m_ref[...] = top
        shrink = jnp.exp(m_in[0] - top)
        l_ref[...] = l_in[0] * shrink
        acc_ref[...] = acc_in[0] * shrink

    count = len(HALO_AT)
    attend(u, 8, count, live_ref, q_ref[0], kv_ref, score_ref, list_ref, m_ref, l_ref, acc_ref, rescale)
    total = jnp.sum(l_ref[...], axis=1, keepdims=True)
    mixed = (acc_ref[...] / total).astype(jnp.bfloat16)
    near_ref[0] = mixed[: TILE // 2]
    far_ref[0] = mixed[TILE // 2 :]


def attend_halo(slab_at, live, q, state, pieces, first, tiles):
    per_u = pl.BlockSpec((1, TILE, HD), lambda r, s_ref, *_: ((first + r) ^ u_base(s_ref[0]), 0, 0))
    count = len(HALO_AT)
    return pl.pallas_call(
        lambda *refs: halo_kernel(first, *refs),
        out_shape=[jax.ShapeDtypeStruct((tiles, TILE // 2, HD), jnp.bfloat16)] * 2,
        grid_spec=pltpu.PrefetchScalarGridSpec(
            num_scalar_prefetch=2,
            grid=(tiles,),
            in_specs=[per_u] * 4 + [pl.BlockSpec(memory_space=pl.ANY)] * len(pieces),
            out_specs=[pl.BlockSpec((1, TILE // 2, HD), lambda r, *_: (r, 0, 0))] * 2,
            scratch_shapes=[
                pltpu.VMEM((count, TILE, 2 * HD), jnp.bfloat16),
                pltpu.VMEM((count, TILE, TILE), jnp.float32),
            ]
            + [pltpu.VMEM((TILE, HD), jnp.float32)] * 3
            + [pltpu.SMEM((count + 1,), jnp.int32), pltpu.SemaphoreType.DMA((len(pieces),))],
        ),
        compiler_params=pltpu.CompilerParams(vmem_limit_bytes=24 << 20),
    )(slab_at, live, q, *state, *pieces)


def output_kernel(s_ref, *refs):
    same, cross, (core_ref, w_ref, wc_ref, wd_ref, gate_ref, out_ref, x_ref, xc_ref, xd_ref) = (
        refs[:4],
        refs[4:8],
        refs[8:],
    )
    s = s_ref[0]
    mine = s & 1

    @pl.when(pl.program_id(0) == 0)
    def _():
        for p in range(4):
            for core, pieces in (
                (mine, (same[p].at[0], cross[p].at[0])),
                (1 - mine, (core_ref.at[p], core_ref.at[4 + p])),
            ):
                slot = slot_of(s, core, p)
                far_ref = xc_ref if core is mine else xd_ref

                @pl.when(slot < 3)
                def _(core=core, slot=slot, pieces=pieces, far_ref=far_ref):
                    x_ref[:, pl.ds(pl.multiple_of((core * 3 + slot) * HD, HD), HD)] = pieces[0][...]
                    far_ref[:, pl.ds(pl.multiple_of(slot * HD, HD), HD)] = pieces[1][...]

    def dot(x, w):
        return jnp.dot(x[...], w[...], preferred_element_type=jnp.float32)

    near = dot(x_ref, w_ref).astype(jnp.bfloat16).astype(jnp.float32)
    far = (dot(xc_ref, wc_ref) + dot(xd_ref, wd_ref)).astype(jnp.bfloat16).astype(jnp.float32)
    out_ref[...] = (gate_ref[...] * (near + far)).astype(jnp.bfloat16)


def output(slab_at, same, cross, core, weight, weight_c, weight_d, gate):
    inner, width = weight.shape
    half = TILE // 2
    cols = 1024
    by_col = lambda rows: pl.BlockSpec((rows, cols), lambda n, s_ref: (0, n))
    return pl.pallas_call(
        output_kernel,
        out_shape=jax.ShapeDtypeStruct((half, width), jnp.bfloat16),
        grid_spec=pltpu.PrefetchScalarGridSpec(
            num_scalar_prefetch=1,
            grid=(width // cols,),
            in_specs=[whole((1, half, HD))] * 8
            + [whole((8, half, HD)), by_col(inner), by_col(inner // 2), by_col(inner // 2), by_col(1)],
            out_specs=by_col(half),
            scratch_shapes=[
                pltpu.VMEM((half, inner), jnp.bfloat16),
                pltpu.VMEM((half, inner // 2), jnp.bfloat16),
                pltpu.VMEM((half, inner // 2), jnp.bfloat16),
            ],
        ),
        compiler_params=pltpu.CompilerParams(vmem_limit_bytes=14 << 20),
        name="output",
    )(slab_at, *same, *cross, core, weight, weight_c, weight_d, gate)


def on_device(
    tokens,
    qkv_weight,
    out_weight,
    query_gain,
    key_gain,
    mod_shift,
    mod_scale,
    branch_gate,
    block_mask,
):
    slab_at = lax.axis_index("slab").astype(jnp.int32).reshape(1)
    own = modulate(tokens, mod_shift, mod_scale)
    far = to_group(own)
    mask_rows = jnp.pad(
        jnp.broadcast_to(block_mask.astype(jnp.bfloat16), (MASK_ROWS, 27)), ((0, 0), (0, 3 * HD - 27))
    )
    gains = (query_gain.reshape(1, HD), key_gain.reshape(1, HD))
    part = weight_part(slab_at, out_weight)
    halves = []
    x = own
    for at in range(2):
        send = project(slab_at, x, qkv_weight, *gains, mask_rows, 1, at == 0)
        if at:
            send, part = lax.optimization_barrier((send, part))
        core = to_core(send)
        keep = project(slab_at, x, qkv_weight, *gains, mask_rows, 0, at == 0)
        near = []
        for p in (1, 2, 3):
            near.append(to_chip(jnp.stack([keep[p], core[p]]), p))
        x = far
        halves.append((keep, core, *near))
    weight_c = weight_across(part)
    q, kv, live, *sends = assemble(slab_at, halves)
    halo = []
    for piece, (moved, _) in zip(sends, HALO):
        halo.append(to_block(piece, moved))
    halo += [None] * 3
    state = attend_own(live, q, kv)
    *state, over = lax.optimization_barrier((*state, halo[2]))
    halo[2] = over
    for at, moved, us in ((4, (0, 0, 1), (0, 2)), (5, (0, 1, 0), (0, 1)), (6, (0, 1, 1), (0,))):
        halo[at] = to_block(jnp.stack([over[u] for u in us]), moved)
    done = {}
    for first, tiles in ((2, 6), (0, 2)):
        mixed, crossing = attend_halo(slab_at, live, q, state, halo, first, tiles)
        if not first:
            mixed, weight_c = lax.optimization_barrier((mixed, weight_c))
        crossed = across(crossing)
        for p in range(first // 2, (first + tiles) // 2):
            r = slice(2 * p - first, 2 * p - first + 2)
            done[p] = (mixed[r], crossed[r])
    weight_d = to_core(weight_c)
    for p in (3, 2, 1):
        moved = from_chip(jnp.concatenate(done[p]), p)
        done[p] = (moved[:2], moved[2:])
    same, cross = zip(*(done[p] for p in range(4)), strict=True)
    core = to_core(jnp.stack([piece[1] for piece in same + cross]))
    gate = branch_gate.reshape(1, -1)
    return output(slab_at, same, cross, core, out_weight, weight_c, weight_d, gate)[None]


def solution(mesh):
    in_specs = (
        P("slab", "heads", None),
        P(None, "heads"),
        P("heads", None),
        P(),
        P(),
        P(),
        P(),
        P(),
        P("slab", None),
    )
    out_specs = P("slab", "heads", None)
    return jax.shard_map(
        on_device,
        mesh=mesh,
        in_specs=in_specs,
        out_specs=out_specs,
        check_vma=False,
    )
```

```python
import jax
import jax.numpy as jnp
import numpy as np
from jax import lax
from jax.experimental import pallas as pl
from jax.experimental.pallas import tpu as pltpu
from jax.sharding import PartitionSpec as P


TILE = 384
HD = 128
MASK_ROWS = 16
NEG = -1e30

HALO = (
    ((0, 0, 1), (0, 2, 4, 6)),
    ((0, 1, 0), (0, 1, 4, 5)),
    ((1, 0, 0), (0, 1, 2, 3)),
    ((1, 0, 1), (0, 2)),
    ((1, 1, 0), (0, 1)),
    ((0, 1, 1), (0, 4)),
    ((1, 1, 1), (0,)),
)
OWN_AT = [((u >> 2) & 1, (u >> 1) & 1, u & 1) for u in range(8)]
HALO_AT = [
    tuple(-1 if moved[d] else ((u >> (2 - d)) & 1) for d in range(3)) for moved, us in HALO for u in us
]


def chip_of(s):
    return ((s >> 4) & 1) * 2 + ((s >> 2) & 1)


def corner_of(s):
    return ((s >> 3) & 1) * 2 + ((s >> 1) & 1)


def slot_of(s, core, p):
    return chip_of(s) ^ p ^ (core * corner_of(s))


def u_base(s):
    ut = ((s >> 4) ^ (s >> 5) ^ 1) & 1
    uh = ((s >> 2) ^ (s >> 3) ^ 1) & 1
    uw = (s ^ (s >> 1) ^ 1) & 1
    return ut * 4 + uh * 2 + uw


def chip_mask(p):
    return ((p >> 1) << 4) | ((p & 1) << 2)


def halo_mask(core, moved):
    mask = (moved[0] << 5) | (moved[1] << 3) | (moved[2] << 1)
    if core:
        mask |= (moved[1] << 4) | (moved[2] << 2)
    return mask


def busy(s):
    return slot_of(s, s & 1, 0) < 3


def to_chip(value, p):
    pairs = [(s, s ^ chip_mask(p)) for s in range(64) if busy(s ^ chip_mask(p))]
    return lax.ppermute(value, "slab", pairs)


def from_chip(value, p):
    pairs = [(s, s ^ chip_mask(p)) for s in range(64) if busy(s)]
    return lax.ppermute(value, "slab", pairs)


def across(value):
    pairs = [(64 * g + s, 64 * (1 - g) + s) for g in range(2) for s in range(64) if busy(s)]
    return lax.ppermute(value, ("heads", "slab"), pairs)


def weight_across(value):
    pairs = [(64 * g + s, 64 * (1 - g) + (s ^ 32)) for g in range(2) for s in range(64)]
    return lax.ppermute(value, ("heads", "slab"), pairs)


def to_core(value):
    return lax.ppermute(value, "slab", [(s, s ^ 1) for s in range(64)])


def to_block(value, moved):
    pairs = [(s, s ^ halo_mask(s & 1, moved)) for s in range(64) if busy(s)]
    return lax.ppermute(value, "slab", pairs)


def to_group(value):
    return lax.ppermute(value, "heads", [(0, 1), (1, 0)])


def whole(shape):
    return pl.BlockSpec(shape, lambda *_: (0,) * len(shape), pipeline_mode=pl.Buffered(1))


def modulate_kernel(x_ref, shift_ref, scale_ref, out_ref):
    rows = x_ref[0].astype(jnp.float32)
    centered = rows - jnp.mean(rows, axis=-1, keepdims=True)
    variance = jnp.mean(centered * centered, axis=-1, keepdims=True)
    out = centered * lax.rsqrt(variance + 1e-06) * (1.0 + scale_ref[...]) + shift_ref[...]
    out_ref[...] = out.astype(jnp.bfloat16)


def modulate(tokens, mod_shift, mod_scale):
    _, rows, width = tokens.shape
    step = 48
    return pl.pallas_call(
        modulate_kernel,
        out_shape=jax.ShapeDtypeStruct((rows, width), jnp.bfloat16),
        grid=(rows // step,),
        in_specs=[
            pl.BlockSpec((1, step, width), lambda i: (0, i, 0)),
            whole((1, width)),
            whole((1, width)),
        ],
        out_specs=pl.BlockSpec((step, width), lambda i: (i, 0)),
        compiler_params=pltpu.CompilerParams(vmem_limit_bytes=8 << 20),
        name="modulate",
    )(tokens, mod_shift.reshape(1, width), mod_scale.reshape(1, width))


def project_kernel(other, s_ref, x_ref, w_ref, qg_ref, kg_ref, mask_ref, out_ref):
    s = s_ref[0]
    rows = x_ref.shape[0]
    slot = slot_of(s, (s & 1) ^ other, pl.program_id(0))

    @pl.when(slot < 3)
    def _():
        acc = jnp.dot(x_ref[...], w_ref[...], preferred_element_type=jnp.float32).astype(jnp.bfloat16)

        def normed(part, gain):
            part = part.astype(jnp.float32)
            return part * lax.rsqrt(jnp.mean(part * part, axis=-1, keepdims=True) + 1e-06) * gain

        q = normed(acc[:, :HD], qg_ref[...]) * HD ** (-0.5)
        out_ref[0, :rows, :HD] = q.astype(jnp.bfloat16)
        out_ref[0, :rows, HD : 2 * HD] = normed(acc[:, HD : 2 * HD], kg_ref[...]).astype(jnp.bfloat16)
        out_ref[0, :rows, 2 * HD :] = acc[:, 2 * HD :]
        if out_ref.shape[1] > rows:
            out_ref[0, rows:, :] = mask_ref[...]

    @pl.when(slot >= 3)
    def _():
        out_ref[0] = jnp.zeros_like(out_ref[0])


def project(slab_at, x, weight, query_gain, key_gain, mask_rows, other, with_mask):
    rows, width = x.shape
    out_rows = rows + (MASK_ROWS if with_mask else 0)

    def weight_at(i, s_ref):
        s = s_ref[0]
        core = (s & 1) ^ other
        return (0, core * 3 + jnp.minimum(slot_of(s, core, i), 2))

    return pl.pallas_call(
        lambda *refs: project_kernel(other, *refs),
        out_shape=jax.ShapeDtypeStruct((4, out_rows, 3 * HD), jnp.bfloat16),
        grid_spec=pltpu.PrefetchScalarGridSpec(
            num_scalar_prefetch=1,
            grid=(4,),
            in_specs=[
                whole((rows, width)),
                pl.BlockSpec((width, 3 * HD), weight_at),
                whole((1, HD)),
                whole((1, HD)),
                whole((MASK_ROWS, 3 * HD)),
            ],
            out_specs=pl.BlockSpec((1, out_rows, 3 * HD), lambda i, s_ref: (i, 0, 0)),
        ),
        compiler_params=pltpu.CompilerParams(vmem_limit_bytes=7 << 20),
    )(slab_at, x, weight, query_gain, key_gain, mask_rows)


def live_tables():
    table = np.full((8, 8, HD), HD, np.int32)
    for corner in range(8):
        signs = [((corner >> (2 - d)) & 1) * 2 - 1 for d in range(3)]
        for u in range(8):
            for k, at in enumerate(OWN_AT + HALO_AT):
                steps = [at[d] - ((u >> (2 - d)) & 1) for d in range(3)]
                if min(steps) >= -1:
                    table[corner, u, k] = 13 + sum(
                        w * g * t for w, g, t in zip((9, 3, 1), signs, steps, strict=True)
                    )
    return table


def block_of(s):
    return ((s >> 5) & 1) * 4 + corner_of(s)


def part_kernel(s_ref, w_ref, out_ref, sem):
    rows = out_ref.shape[0]
    start = pl.multiple_of((s_ref[0] & 1) * rows, rows)
    copy = pltpu.make_async_copy(w_ref.at[pl.ds(start, rows)], out_ref, sem)
    copy.start()
    copy.wait()


def weight_part(slab_at, weight):
    rows, width = weight.shape
    return pl.pallas_call(
        part_kernel,
        out_shape=jax.ShapeDtypeStruct((rows // 2, width), weight.dtype),
        grid_spec=pltpu.PrefetchScalarGridSpec(
            num_scalar_prefetch=1,
            grid=(1,),
            in_specs=[pl.BlockSpec(memory_space=pl.ANY)],
            out_specs=pl.BlockSpec(memory_space=pl.ANY),
            scratch_shapes=[pltpu.SemaphoreType.DMA(())],
        ),
        compiler_params=pltpu.CompilerParams(vmem_limit_bytes=1 << 20),
        name="weight_part",
    )(slab_at, weight)


def assemble_kernel(s_ref, *refs):
    base = u_base(s_ref[0])
    half = TILE // 2
    spot_ref, q_ref, kv_ref, live_ref = refs[10:14]
    entry = lax.broadcasted_iota(jnp.int32, (HD, HD), 0)
    lane = lax.broadcasted_iota(jnp.int32, (MASK_ROWS, HD), 1)
    for at, halves in enumerate((refs[:5], refs[5:10])):
        keep_ref, core_ref, *near = halves
        pieces = [(keep_ref, 0), (core_ref, 0)] + [(ref, dc) for ref in near for dc in range(2)]
        rows = slice(at * half, (at + 1) * half)
        for r, (ref, dc) in enumerate(pieces):
            u = base ^ r
            q_ref[u, rows] = ref[dc, :half, :HD]
            kv_ref[u, rows] = ref[dc, :half, HD:]
            if at == 0:
                marked = jnp.where(lane == 13, 1.0, ref[dc, half:, :HD].astype(jnp.float32))
                pick = jnp.where(entry == spot_ref[0, pl.ds(u, 1)], 1.0, 0.0)
                live = jnp.dot(
                    marked.astype(jnp.bfloat16),
                    pick.astype(jnp.bfloat16),
                    preferred_element_type=jnp.float32,
                )
                live_ref[pl.ds(u, 1)] = live[:1].astype(jnp.int32)
    for (_, us), send in zip(HALO, refs[14:]):
        for at, u in enumerate(us):
            send[at] = kv_ref[u]


def assemble(slab_at, halves):
    shapes = [
        ((8, TILE, HD), jnp.bfloat16),
        ((8, TILE, 2 * HD), jnp.bfloat16),
        ((8, HD), jnp.int32),
    ] + [((len(us), TILE, 2 * HD), jnp.bfloat16) for _, us in HALO[:3]]
    in_specs = []
    for keep, *_ in halves:
        rows = keep.shape[1]
        in_specs += [whole((1, rows, 3 * HD))] * 2 + [whole((2, rows, 3 * HD))] * 3
    in_specs.append(pl.BlockSpec((1, 8, HD), lambda i, s_ref: (block_of(s_ref[0]), 0, 0)))
    return pl.pallas_call(
        assemble_kernel,
        out_shape=[jax.ShapeDtypeStruct(*shape) for shape in shapes],
        grid_spec=pltpu.PrefetchScalarGridSpec(
            num_scalar_prefetch=1,
            grid=(1,),
            in_specs=in_specs,
            out_specs=[whole(shape) for shape, _ in shapes],
        ),
        compiler_params=pltpu.CompilerParams(vmem_limit_bytes=16 << 20),
        name="assemble",
    )(slab_at, *halves[0], *halves[1], jnp.asarray(live_tables()))


def fold(x, op):
    return op(op(x[:, :HD], x[:, HD : 2 * HD]), x[:, 2 * HD :])


def spread_max(x):
    return jnp.broadcast_to(jnp.max(x, axis=1, keepdims=True), x.shape)


def attend(u, first, count, live_ref, q, kv_ref, s_ref, list_ref, m_ref, l_ref, acc_ref, rescale):
    n = jnp.int32(0)
    for k in range(count):
        list_ref[n] = k
        n = n + live_ref[u, first + k]

    def score(base, group):
        def step(j, _):
            top = m_ref[...]
            for i in range(group):
                at = base + j * group + i
                scores = lax.dot_general(
                    q,
                    kv_ref[list_ref[at], :, :HD],
                    (((1,), (1,)), ((), ())),
                    preferred_element_type=jnp.float32,
                )
                s_ref[at] = scores
                top = jnp.maximum(top, fold(scores, jnp.maximum))
            m_ref[...] = top
            return 0

        return step

    def weigh(base, group):
        def step(j, _):
            top = m_ref[...]
            top = jnp.concatenate([top, top, top], axis=1)
            total = l_ref[...]
            acc = acc_ref[...]
            for i in range(group):
                at = base + j * group + i
                raised = jnp.exp(s_ref[at] - top)
                total = total + fold(raised, jnp.add)
                acc = acc + jnp.dot(
                    raised.astype(jnp.bfloat16),
                    kv_ref[list_ref[at], :, HD:],
                    preferred_element_type=jnp.float32,
                )
            l_ref[...] = total
            acc_ref[...] = acc
            return 0

        return step

    def each(make):
        lax.fori_loop(0, n >> 2, make(0, 4), 0)
        lax.fori_loop(0, (n >> 1) & 1, make((n >> 2) << 2, 2), 0)
        lax.fori_loop(0, n & 1, make((n >> 1) << 1, 1), 0)

    each(score)
    rescale(spread_max(m_ref[...]))
    each(weigh)


def own_kernel(first, live_ref, q_ref, kv_ref, *refs):
    u = first + pl.program_id(0)
    m_ref, l_ref, acc_ref, s_ref, list_ref = refs[-5:]
    m, l, acc = m_ref.at[0], l_ref.at[0], acc_ref.at[0]
    m[...] = jnp.full_like(m[...], NEG)

    def rescale(top):
        m[...] = top
        l[...] = jnp.zeros_like(l[...])
        acc[...] = jnp.zeros_like(acc[...])

    attend(u, 0, 8, live_ref, q_ref[0], kv_ref, s_ref, list_ref, m, l, acc, rescale)


def attend_own(live, q, kv, first, tiles, prior):
    per_u = pl.BlockSpec((1, TILE, HD), lambda u, *_: (first + u, 0, 0))
    state = jax.ShapeDtypeStruct((8, TILE, HD), jnp.float32)
    return pl.pallas_call(
        lambda *refs: own_kernel(first, *refs),
        out_shape=[state, state, state],
        grid_spec=pltpu.PrefetchScalarGridSpec(
            num_scalar_prefetch=1,
            grid=(tiles,),
            in_specs=[per_u, whole((8, TILE, 2 * HD))]
            + [pl.BlockSpec(memory_space=pl.ANY)] * len(prior),
            out_specs=[per_u] * 3,
            scratch_shapes=[pltpu.VMEM((8, TILE, TILE), jnp.float32), pltpu.SMEM((9,), jnp.int32)],
        ),
        input_output_aliases={3 + i: i for i in range(len(prior))},
        compiler_params=pltpu.CompilerParams(vmem_limit_bytes=14 << 20),
    )(live, q, kv, *prior)


def halo_kernel(first, s_ref, live_ref, q_ref, m_in, l_in, acc_in, *refs):
    pieces, (near_ref, far_ref, kv_ref, score_ref, m_ref, l_ref, acc_ref, list_ref, sems) = refs[:6], refs[6:]

    @pl.when(pl.program_id(0) == 0)
    def _():
        at = 0
        copies = []
        for i, piece in enumerate(pieces):
            to = kv_ref.at[pl.ds(at, piece.shape[0])]
            copies.append(pltpu.make_async_copy(piece, to, sems.at[i]))
            at += piece.shape[0]
        for copy in copies:
            copy.start()
        for copy in copies:
            copy.wait()

    u = (first + pl.program_id(0)) ^ u_base(s_ref[0])
    m_ref[...] = m_in[0]

    def rescale(top):
        m_ref[...] = top
        shrink = jnp.exp(m_in[0] - top)
        l_ref[...] = l_in[0] * shrink
        acc_ref[...] = acc_in[0] * shrink

    count = len(HALO_AT)
    attend(u, 8, count, live_ref, q_ref[0], kv_ref, score_ref, list_ref, m_ref, l_ref, acc_ref, rescale)
    total = jnp.sum(l_ref[...], axis=1, keepdims=True)
    mixed = (acc_ref[...] / total).astype(jnp.bfloat16)
    near_ref[0] = mixed[: TILE // 2]
    far_ref[0] = mixed[TILE // 2 :]


def attend_halo(slab_at, live, q, state, pieces, first, tiles):
    per_u = pl.BlockSpec((1, TILE, HD), lambda r, s_ref, *_: ((first + r) ^ u_base(s_ref[0]), 0, 0))
    count = len(HALO_AT)
    return pl.pallas_call(
        lambda *refs: halo_kernel(first, *refs),
        out_shape=[jax.ShapeDtypeStruct((tiles, TILE // 2, HD), jnp.bfloat16)] * 2,
        grid_spec=pltpu.PrefetchScalarGridSpec(
            num_scalar_prefetch=2,
            grid=(tiles,),
            in_specs=[per_u] * 4 + [pl.BlockSpec(memory_space=pl.ANY)] * len(pieces),
            out_specs=[pl.BlockSpec((1, TILE // 2, HD), lambda r, *_: (r, 0, 0))] * 2,
            scratch_shapes=[
                pltpu.VMEM((count, TILE, 2 * HD), jnp.bfloat16),
                pltpu.VMEM((count, TILE, TILE), jnp.float32),
            ]
            + [pltpu.VMEM((TILE, HD), jnp.float32)] * 3
            + [pltpu.SMEM((count + 1,), jnp.int32), pltpu.SemaphoreType.DMA((len(pieces),))],
        ),
        compiler_params=pltpu.CompilerParams(vmem_limit_bytes=24 << 20),
    )(slab_at, live, q, *state, *pieces)


def output_kernel(s_ref, *refs):
    same, cross, (core_ref, w_ref, wc_ref, wd_ref, gate_ref, out_ref, x_ref, xc_ref, xd_ref) = (
        refs[:4],
        refs[4:8],
        refs[8:],
    )
    s = s_ref[0]
    mine = s & 1

    @pl.when(pl.program_id(0) == 0)
    def _():
        for p in range(4):
            for core, pieces in (
                (mine, (same[p].at[0], cross[p].at[0])),
                (1 - mine, (core_ref.at[p], core_ref.at[4 + p])),
            ):
                slot = slot_of(s, core, p)
                far_ref = xc_ref if core is mine else xd_ref

                @pl.when(slot < 3)
                def _(core=core, slot=slot, pieces=pieces, far_ref=far_ref):
                    x_ref[:, pl.ds(pl.multiple_of((core * 3 + slot) * HD, HD), HD)] = pieces[0][...]
                    far_ref[:, pl.ds(pl.multiple_of(slot * HD, HD), HD)] = pieces[1][...]

    def dot(x, w):
        return jnp.dot(x[...], w[...], preferred_element_type=jnp.float32)

    near = dot(x_ref, w_ref).astype(jnp.bfloat16).astype(jnp.float32)
    far = (dot(xc_ref, wc_ref) + dot(xd_ref, wd_ref)).astype(jnp.bfloat16).astype(jnp.float32)
    out_ref[...] = (gate_ref[...] * (near + far)).astype(jnp.bfloat16)


def output(slab_at, same, cross, core, weight, weight_c, weight_d, gate):
    inner, width = weight.shape
    half = TILE // 2
    cols = 512
    by_col = lambda rows: pl.BlockSpec((rows, cols), lambda n, s_ref: (0, n))
    return pl.pallas_call(
        output_kernel,
        out_shape=jax.ShapeDtypeStruct((half, width), jnp.bfloat16),
        grid_spec=pltpu.PrefetchScalarGridSpec(
            num_scalar_prefetch=1,
            grid=(width // cols,),
            in_specs=[whole((1, half, HD))] * 8
            + [whole((8, half, HD)), by_col(inner), by_col(inner // 2), by_col(inner // 2), by_col(1)],
            out_specs=by_col(half),
            scratch_shapes=[
                pltpu.VMEM((half, inner), jnp.bfloat16),
                pltpu.VMEM((half, inner // 2), jnp.bfloat16),
                pltpu.VMEM((half, inner // 2), jnp.bfloat16),
            ],
        ),
        compiler_params=pltpu.CompilerParams(vmem_limit_bytes=14 << 20),
        name="output",
    )(slab_at, *same, *cross, core, weight, weight_c, weight_d, gate)


def on_device(
    tokens,
    qkv_weight,
    out_weight,
    query_gain,
    key_gain,
    mod_shift,
    mod_scale,
    branch_gate,
    block_mask,
):
    slab_at = lax.axis_index("slab").astype(jnp.int32).reshape(1)
    own = modulate(tokens, mod_shift, mod_scale)
    far = to_group(own)
    mask_rows = jnp.pad(
        jnp.broadcast_to(block_mask.astype(jnp.bfloat16), (MASK_ROWS, 27)), ((0, 0), (0, 3 * HD - 27))
    )
    gains = (query_gain.reshape(1, HD), key_gain.reshape(1, HD))
    part = weight_part(slab_at, out_weight)
    halves = []
    x = own
    for at in range(2):
        send = project(slab_at, x, qkv_weight, *gains, mask_rows, 1, at == 0)
        if at:
            send, part = lax.optimization_barrier((send, part))
        core = to_core(send)
        keep = project(slab_at, x, qkv_weight, *gains, mask_rows, 0, at == 0)
        near = []
        for p in (1, 2, 3):
            near.append(to_chip(jnp.stack([keep[p], core[p]]), p))
        x = far
        halves.append((keep, core, *near))
    weight_c = weight_across(part)
    q, kv, live, *sends = assemble(slab_at, halves)
    halo = []
    for piece, (moved, _) in zip(sends, HALO):
        halo.append(to_block(piece, moved))
    state = attend_own(live, q, kv, 0, 4, ())
    *state, side, over = lax.optimization_barrier((*state, halo[0], halo[2]))
    halo = [side, halo[1], over]
    for moved, tiles in (
        ((0, 0, 1), (over[0], over[2])), ((0, 1, 0), (over[0], over[1], side[0], side[2])), ((0, 1, 1), (over[0],))
    ):
        halo.append(to_block(jnp.stack(tiles), moved))
    state = attend_own(live, q, kv, 4, 4, state)
    done = {}
    for first, tiles in ((2, 6), (0, 2)):
        mixed, crossing = attend_halo(slab_at, live, q, state, halo, first, tiles)
        if not first:
            mixed, weight_c = lax.optimization_barrier((mixed, weight_c))
        crossed = across(crossing)
        for p in range(first // 2, (first + tiles) // 2):
            r = slice(2 * p - first, 2 * p - first + 2)
            done[p] = (mixed[r], crossed[r])
    weight_d = to_core(weight_c)
    for p in (3, 2, 1):
        moved = from_chip(jnp.concatenate(done[p]), p)
        done[p] = (moved[:2], moved[2:])
    same, cross = zip(*(done[p] for p in range(4)), strict=True)
    core = to_core(jnp.stack([piece[1] for piece in same + cross]))
    gate = branch_gate.reshape(1, -1)
    return output(slab_at, same, cross, core, out_weight, weight_c, weight_d, gate)[None]


def solution(mesh):
    in_specs = (
        P("slab", "heads", None),
        P(None, "heads"),
        P("heads", None),
        P(),
        P(),
        P(),
        P(),
        P(),
        P("slab", None),
    )
    out_specs = P("slab", "heads", None)
    return jax.shard_map(
        on_device,
        mesh=mesh,
        in_specs=in_specs,
        out_specs=out_specs,
        check_vma=False,
    )
```

```python
import jax
import jax.numpy as jnp
import numpy as np
from jax import lax
from jax.experimental import pallas as pl
from jax.experimental.pallas import tpu as pltpu
from jax.sharding import PartitionSpec as P


TILE = 384
HD = 128
MASK_ROWS = 16
NEG = -1e30

HALO = (
    ((0, 0, 1), (0, 2, 4, 6)),
    ((0, 1, 0), (0, 1, 4, 5)),
    ((1, 0, 0), (0, 1, 2, 3)),
    ((1, 0, 1), (0, 2)),
    ((1, 1, 0), (0, 1)),
    ((0, 1, 1), (0, 4)),
    ((1, 1, 1), (0,)),
)
OWN_AT = [((u >> 2) & 1, (u >> 1) & 1, u & 1) for u in range(8)]
HALO_AT = [
    tuple(-1 if moved[d] else ((u >> (2 - d)) & 1) for d in range(3)) for moved, us in HALO for u in us
]


def chip_of(s):
    return ((s >> 4) & 1) * 2 + ((s >> 2) & 1)


def corner_of(s):
    return ((s >> 3) & 1) * 2 + ((s >> 1) & 1)


def slot_of(s, core, p):
    return chip_of(s) ^ p ^ (core * corner_of(s))


def u_base(s):
    ut = ((s >> 4) ^ (s >> 5) ^ 1) & 1
    uh = ((s >> 2) ^ (s >> 3) ^ 1) & 1
    uw = (s ^ (s >> 1) ^ 1) & 1
    return ut * 4 + uh * 2 + uw


def chip_mask(p):
    return ((p >> 1) << 4) | ((p & 1) << 2)


def halo_mask(core, moved):
    mask = (moved[0] << 5) | (moved[1] << 3) | (moved[2] << 1)
    if core:
        mask |= (moved[1] << 4) | (moved[2] << 2)
    return mask


def busy(s):
    return slot_of(s, s & 1, 0) < 3


def to_chip(value, p):
    pairs = [(s, s ^ chip_mask(p)) for s in range(64) if busy(s ^ chip_mask(p))]
    return lax.ppermute(value, "slab", pairs)


def from_chip(value, p):
    pairs = [(s, s ^ chip_mask(p)) for s in range(64) if busy(s)]
    return lax.ppermute(value, "slab", pairs)


def across(value):
    pairs = [(64 * g + s, 64 * (1 - g) + s) for g in range(2) for s in range(64) if busy(s)]
    return lax.ppermute(value, ("heads", "slab"), pairs)


def weight_across(value):
    pairs = [(64 * g + s, 64 * (1 - g) + (s ^ 32)) for g in range(2) for s in range(64)]
    return lax.ppermute(value, ("heads", "slab"), pairs)


def to_core(value):
    return lax.ppermute(value, "slab", [(s, s ^ 1) for s in range(64)])


def to_block(value, moved):
    pairs = [(s, s ^ halo_mask(s & 1, moved)) for s in range(64) if busy(s)]
    return lax.ppermute(value, "slab", pairs)


def to_group(value):
    return lax.ppermute(value, "heads", [(0, 1), (1, 0)])


def whole(shape):
    return pl.BlockSpec(shape, lambda *_: (0,) * len(shape), pipeline_mode=pl.Buffered(1))


def modulate_kernel(x_ref, shift_ref, scale_ref, out_ref):
    rows = x_ref[0].astype(jnp.float32)
    centered = rows - jnp.mean(rows, axis=-1, keepdims=True)
    variance = jnp.mean(centered * centered, axis=-1, keepdims=True)
    out = centered * lax.rsqrt(variance + 1e-06) * (1.0 + scale_ref[...]) + shift_ref[...]
    out_ref[...] = out.astype(jnp.bfloat16)


def modulate(tokens, mod_shift, mod_scale):
    _, rows, width = tokens.shape
    step = 48
    return pl.pallas_call(
        modulate_kernel,
        out_shape=jax.ShapeDtypeStruct((rows, width), jnp.bfloat16),
        grid=(rows // step,),
        in_specs=[
            pl.BlockSpec((1, step, width), lambda i: (0, i, 0)),
            whole((1, width)),
            whole((1, width)),
        ],
        out_specs=pl.BlockSpec((step, width), lambda i: (i, 0)),
        compiler_params=pltpu.CompilerParams(vmem_limit_bytes=8 << 20),
        name="modulate",
    )(tokens, mod_shift.reshape(1, width), mod_scale.reshape(1, width))


def project_kernel(other, s_ref, x_ref, w_ref, qg_ref, kg_ref, mask_ref, out_ref):
    s = s_ref[0]
    rows = x_ref.shape[0]
    core = (s & 1) ^ other

    def normed(part, gain):
        part = part.astype(jnp.float32)
        return part * lax.rsqrt(jnp.mean(part * part, axis=-1, keepdims=True) + 1e-06) * gain

    def one_slot(i, _):
        slot = slot_of(s, core, i)

        @pl.when(slot < 3)
        def _():
            at = pl.multiple_of((core * 3 + slot) * (3 * HD), 3 * HD)
            acc = jnp.dot(
                x_ref[...], w_ref[:, pl.ds(at, 3 * HD)], preferred_element_type=jnp.float32
            ).astype(jnp.bfloat16)
            q = normed(acc[:, :HD], qg_ref[...]) * HD ** (-0.5)
            out_ref[i, :rows, :HD] = q.astype(jnp.bfloat16)
            out_ref[i, :rows, HD : 2 * HD] = normed(acc[:, HD : 2 * HD], kg_ref[...]).astype(
                jnp.bfloat16
            )
            out_ref[i, :rows, 2 * HD :] = acc[:, 2 * HD :]
            if out_ref.shape[1] > rows:
                out_ref[i, rows:, :] = mask_ref[...]

        @pl.when(slot >= 3)
        def _():
            out_ref[i] = jnp.zeros_like(out_ref[i])

        return 0

    lax.fori_loop(0, 4, one_slot, 0)


def project(slab_at, x, weight, query_gain, key_gain, mask_rows, other, with_mask):
    rows, _ = x.shape
    out_rows = rows + (MASK_ROWS if with_mask else 0)
    vmem = pl.BlockSpec(memory_space=pltpu.VMEM)
    return pl.pallas_call(
        lambda *refs: project_kernel(other, *refs),
        out_shape=jax.ShapeDtypeStruct((4, out_rows, 3 * HD), jnp.bfloat16),
        in_specs=[pl.BlockSpec(memory_space=pltpu.SMEM)] + [vmem] * 5,
        out_specs=vmem,
        compiler_params=pltpu.CompilerParams(vmem_limit_bytes=20 << 20),
    )(slab_at, x, weight, query_gain, key_gain, mask_rows)


def live_tables():
    table = np.full((8, 8, HD), HD, np.int32)
    for corner in range(8):
        signs = [((corner >> (2 - d)) & 1) * 2 - 1 for d in range(3)]
        for u in range(8):
            for k, at in enumerate(OWN_AT + HALO_AT):
                steps = [at[d] - ((u >> (2 - d)) & 1) for d in range(3)]
                if min(steps) >= -1:
                    table[corner, u, k] = 13 + sum(
                        w * g * t for w, g, t in zip((9, 3, 1), signs, steps, strict=True)
                    )
    return table


def block_of(s):
    return ((s >> 5) & 1) * 4 + corner_of(s)


def part_kernel(s_ref, w_ref, out_ref, sem):
    rows = out_ref.shape[0]
    start = pl.multiple_of((s_ref[0] & 1) * rows, rows)
    copy = pltpu.make_async_copy(w_ref.at[pl.ds(start, rows)], out_ref, sem)
    copy.start()
    copy.wait()


def weight_part(slab_at, weight):
    rows, width = weight.shape
    return pl.pallas_call(
        part_kernel,
        out_shape=jax.ShapeDtypeStruct((rows // 2, width), weight.dtype),
        grid_spec=pltpu.PrefetchScalarGridSpec(
            num_scalar_prefetch=1,
            grid=(1,),
            in_specs=[pl.BlockSpec(memory_space=pl.ANY)],
            out_specs=pl.BlockSpec(memory_space=pl.ANY),
            scratch_shapes=[pltpu.SemaphoreType.DMA(())],
        ),
        compiler_params=pltpu.CompilerParams(vmem_limit_bytes=1 << 20),
        name="weight_part",
    )(slab_at, weight)


def assemble_kernel(s_ref, *refs):
    base = u_base(s_ref[0])
    half = TILE // 2
    spot_ref, q_ref, kv_ref, live_ref = refs[10:14]
    entry = lax.broadcasted_iota(jnp.int32, (HD, HD), 0)
    lane = lax.broadcasted_iota(jnp.int32, (MASK_ROWS, HD), 1)
    for at, halves in enumerate((refs[:5], refs[5:10])):
        keep_ref, core_ref, *near = halves
        pieces = [(keep_ref, 0), (core_ref, 0)] + [(ref, dc) for ref in near for dc in range(2)]
        rows = slice(at * half, (at + 1) * half)
        for r, (ref, dc) in enumerate(pieces):
            u = base ^ r
            q_ref[u, rows] = ref[dc, :half, :HD]
            kv_ref[u, rows] = ref[dc, :half, HD:]
            if at == 0:
                marked = jnp.where(lane == 13, 1.0, ref[dc, half:, :HD].astype(jnp.float32))
                pick = jnp.where(entry == spot_ref[0, pl.ds(u, 1)], 1.0, 0.0)
                live = jnp.dot(
                    marked.astype(jnp.bfloat16),
                    pick.astype(jnp.bfloat16),
                    preferred_element_type=jnp.float32,
                )
                live_ref[pl.ds(u, 1)] = live[:1].astype(jnp.int32)
    for (_, us), send in zip(HALO, refs[14:]):
        for at, u in enumerate(us):
            send[at] = kv_ref[u]


def assemble(slab_at, halves):
    shapes = [
        ((8, TILE, HD), jnp.bfloat16),
        ((8, TILE, 2 * HD), jnp.bfloat16),
        ((8, HD), jnp.int32),
    ] + [((len(us), TILE, 2 * HD), jnp.bfloat16) for _, us in HALO[:3]]
    in_specs = []
    for keep, *_ in halves:
        rows = keep.shape[1]
        in_specs += [whole((1, rows, 3 * HD))] * 2 + [whole((2, rows, 3 * HD))] * 3
    in_specs.append(pl.BlockSpec((1, 8, HD), lambda i, s_ref: (block_of(s_ref[0]), 0, 0)))
    return pl.pallas_call(
        assemble_kernel,
        out_shape=[jax.ShapeDtypeStruct(*shape) for shape in shapes],
        grid_spec=pltpu.PrefetchScalarGridSpec(
            num_scalar_prefetch=1,
            grid=(1,),
            in_specs=in_specs,
            out_specs=[whole(shape) for shape, _ in shapes],
        ),
        compiler_params=pltpu.CompilerParams(vmem_limit_bytes=16 << 20),
        name="assemble",
    )(slab_at, *halves[0], *halves[1], jnp.asarray(live_tables()))


def fold(x, op):
    return op(op(x[:, :HD], x[:, HD : 2 * HD]), x[:, 2 * HD :])


def spread_max(x):
    return jnp.broadcast_to(jnp.max(x, axis=1, keepdims=True), x.shape)


def attend(u, first, count, live_ref, q, kv_ref, s_ref, list_ref, m_ref, l_ref, acc_ref, rescale):
    n = jnp.int32(0)
    for k in range(count):
        list_ref[n] = k
        n = n + live_ref[u, first + k]

    def score(base, group):
        def step(j, _):
            top = m_ref[...]
            for i in range(group):
                at = base + j * group + i
                scores = lax.dot_general(
                    q,
                    kv_ref[list_ref[at], :, :HD],
                    (((1,), (1,)), ((), ())),
                    preferred_element_type=jnp.float32,
                )
                s_ref[at] = scores
                top = jnp.maximum(top, fold(scores, jnp.maximum))
            m_ref[...] = top
            return 0

        return step

    def weigh(base, group):
        def step(j, _):
            top = m_ref[...]
            top = jnp.concatenate([top, top, top], axis=1)
            total = l_ref[...]
            acc = acc_ref[...]
            for i in range(group):
                at = base + j * group + i
                raised = jnp.exp(s_ref[at] - top)
                total = total + fold(raised, jnp.add)
                acc = acc + jnp.dot(
                    raised.astype(jnp.bfloat16),
                    kv_ref[list_ref[at], :, HD:],
                    preferred_element_type=jnp.float32,
                )
            l_ref[...] = total
            acc_ref[...] = acc
            return 0

        return step

    def each(make):
        lax.fori_loop(0, n >> 2, make(0, 4), 0)
        lax.fori_loop(0, (n >> 1) & 1, make((n >> 2) << 2, 2), 0)
        lax.fori_loop(0, n & 1, make((n >> 1) << 1, 1), 0)

    each(score)
    rescale(spread_max(m_ref[...]))
    each(weigh)


def own_kernel(first, live_ref, q_ref, kv_ref, *refs):
    u = first + pl.program_id(0)
    m_ref, l_ref, acc_ref, s_ref, list_ref = refs[-5:]
    m, l, acc = m_ref.at[0], l_ref.at[0], acc_ref.at[0]
    m[...] = jnp.full_like(m[...], NEG)

    def rescale(top):
        m[...] = top
        l[...] = jnp.zeros_like(l[...])
        acc[...] = jnp.zeros_like(acc[...])

    attend(u, 0, 8, live_ref, q_ref[0], kv_ref, s_ref, list_ref, m, l, acc, rescale)


def attend_own(live, q, kv, first, tiles, prior):
    per_u = pl.BlockSpec((1, TILE, HD), lambda u, *_: (first + u, 0, 0))
    state = jax.ShapeDtypeStruct((8, TILE, HD), jnp.float32)
    return pl.pallas_call(
        lambda *refs: own_kernel(first, *refs),
        out_shape=[state, state, state],
        grid_spec=pltpu.PrefetchScalarGridSpec(
            num_scalar_prefetch=1,
            grid=(tiles,),
            in_specs=[per_u, whole((8, TILE, 2 * HD))]
            + [pl.BlockSpec(memory_space=pl.ANY)] * len(prior),
            out_specs=[per_u] * 3,
            scratch_shapes=[pltpu.VMEM((8, TILE, TILE), jnp.float32), pltpu.SMEM((9,), jnp.int32)],
        ),
        input_output_aliases={3 + i: i for i in range(len(prior))},
        compiler_params=pltpu.CompilerParams(vmem_limit_bytes=14 << 20),
    )(live, q, kv, *prior)


def halo_kernel(first, s_ref, live_ref, q_ref, m_in, l_in, acc_in, *refs):
    pieces, (near_ref, far_ref, kv_ref, score_ref, m_ref, l_ref, acc_ref, list_ref, sems) = refs[:6], refs[6:]

    @pl.when(pl.program_id(0) == 0)
    def _():
        at = 0
        copies = []
        for i, piece in enumerate(pieces):
            to = kv_ref.at[pl.ds(at, piece.shape[0])]
            copies.append(pltpu.make_async_copy(piece, to, sems.at[i]))
            at += piece.shape[0]
        for copy in copies:
            copy.start()
        for copy in copies:
            copy.wait()

    u = (first + pl.program_id(0)) ^ u_base(s_ref[0])
    m_ref[...] = m_in[0]

    def rescale(top):
        m_ref[...] = top
        shrink = jnp.exp(m_in[0] - top)
        l_ref[...] = l_in[0] * shrink
        acc_ref[...] = acc_in[0] * shrink

    count = len(HALO_AT)
    attend(u, 8, count, live_ref, q_ref[0], kv_ref, score_ref, list_ref, m_ref, l_ref, acc_ref, rescale)
    total = jnp.sum(l_ref[...], axis=1, keepdims=True)
    mixed = (acc_ref[...] / total).astype(jnp.bfloat16)
    near_ref[0] = mixed[: TILE // 2]
    far_ref[0] = mixed[TILE // 2 :]


def attend_halo(slab_at, live, q, state, pieces, first, tiles):
    per_u = pl.BlockSpec((1, TILE, HD), lambda r, s_ref, *_: ((first + r) ^ u_base(s_ref[0]), 0, 0))
    count = len(HALO_AT)
    return pl.pallas_call(
        lambda *refs: halo_kernel(first, *refs),
        out_shape=[jax.ShapeDtypeStruct((tiles, TILE // 2, HD), jnp.bfloat16)] * 2,
        grid_spec=pltpu.PrefetchScalarGridSpec(
            num_scalar_prefetch=2,
            grid=(tiles,),
            in_specs=[per_u] * 4 + [pl.BlockSpec(memory_space=pl.ANY)] * len(pieces),
            out_specs=[pl.BlockSpec((1, TILE // 2, HD), lambda r, *_: (r, 0, 0))] * 2,
            scratch_shapes=[
                pltpu.VMEM((count, TILE, 2 * HD), jnp.bfloat16),
                pltpu.VMEM((count, TILE, TILE), jnp.float32),
            ]
            + [pltpu.VMEM((TILE, HD), jnp.float32)] * 3
            + [pltpu.SMEM((count + 1,), jnp.int32), pltpu.SemaphoreType.DMA((len(pieces),))],
        ),
        compiler_params=pltpu.CompilerParams(vmem_limit_bytes=24 << 20),
    )(slab_at, live, q, *state, *pieces)


def output_kernel(s_ref, *refs):
    same, cross, (core_ref, w_ref, wc_ref, wd_ref, gate_ref, out_ref, x_ref, xc_ref, xd_ref) = (
        refs[:4],
        refs[4:8],
        refs[8:],
    )
    s = s_ref[0]
    mine = s & 1

    @pl.when(pl.program_id(0) == 0)
    def _():
        for p in range(4):
            for core, pieces in (
                (mine, (same[p].at[0], cross[p].at[0])),
                (1 - mine, (core_ref.at[p], core_ref.at[4 + p])),
            ):
                slot = slot_of(s, core, p)
                far_ref = xc_ref if core is mine else xd_ref

                @pl.when(slot < 3)
                def _(core=core, slot=slot, pieces=pieces, far_ref=far_ref):
                    x_ref[:, pl.ds(pl.multiple_of((core * 3 + slot) * HD, HD), HD)] = pieces[0][...]
                    far_ref[:, pl.ds(pl.multiple_of(slot * HD, HD), HD)] = pieces[1][...]

    def dot(x, w):
        return jnp.dot(x[...], w[...], preferred_element_type=jnp.float32)

    near = dot(x_ref, w_ref).astype(jnp.bfloat16).astype(jnp.float32)
    far = (dot(xc_ref, wc_ref) + dot(xd_ref, wd_ref)).astype(jnp.bfloat16).astype(jnp.float32)
    out_ref[...] = (gate_ref[...] * (near + far)).astype(jnp.bfloat16)


def output(slab_at, same, cross, core, weight, weight_c, weight_d, gate):
    inner, width = weight.shape
    half = TILE // 2
    cols = 1024
    by_col = lambda rows: pl.BlockSpec((rows, cols), lambda n, s_ref: (0, n))
    return pl.pallas_call(
        output_kernel,
        out_shape=jax.ShapeDtypeStruct((half, width), jnp.bfloat16),
        grid_spec=pltpu.PrefetchScalarGridSpec(
            num_scalar_prefetch=1,
            grid=(width // cols,),
            in_specs=[whole((1, half, HD))] * 8
            + [whole((8, half, HD)), by_col(inner), by_col(inner // 2), by_col(inner // 2), by_col(1)],
            out_specs=by_col(half),
            scratch_shapes=[
                pltpu.VMEM((half, inner), jnp.bfloat16),
                pltpu.VMEM((half, inner // 2), jnp.bfloat16),
                pltpu.VMEM((half, inner // 2), jnp.bfloat16),
            ],
        ),
        compiler_params=pltpu.CompilerParams(vmem_limit_bytes=10 << 20),
        name="output",
    )(slab_at, *same, *cross, core, weight, weight_c, weight_d, gate)


def on_device(
    tokens,
    qkv_weight,
    out_weight,
    query_gain,
    key_gain,
    mod_shift,
    mod_scale,
    branch_gate,
    block_mask,
):
    slab_at = lax.axis_index("slab").astype(jnp.int32).reshape(1)
    own = modulate(tokens, mod_shift, mod_scale)
    far = to_group(own)
    mask_rows = jnp.pad(
        jnp.broadcast_to(block_mask.astype(jnp.bfloat16), (MASK_ROWS, 27)), ((0, 0), (0, 3 * HD - 27))
    )
    gains = (query_gain.reshape(1, HD), key_gain.reshape(1, HD))
    part = weight_part(slab_at, out_weight)
    halves = []
    x = own
    for at in range(2):
        send = project(slab_at, x, qkv_weight, *gains, mask_rows, 1, at == 0)
        if at:
            send, part = lax.optimization_barrier((send, part))
        core = to_core(send)
        keep = project(slab_at, x, qkv_weight, *gains, mask_rows, 0, at == 0)
        near = []
        for p in (1, 2, 3):
            near.append(to_chip(jnp.stack([keep[p], core[p]]), p))
        x = far
        halves.append((keep, core, *near))
    weight_c = weight_across(part)
    q, kv, live, *sends = assemble(slab_at, halves)
    halo = []
    for piece, (moved, _) in zip(sends, HALO):
        halo.append(to_block(piece, moved))
    state = attend_own(live, q, kv, 0, 6, ())
    *state, side, over = lax.optimization_barrier((*state, halo[0], halo[2]))
    halo = [side, halo[1], over]
    for moved, tiles in (
        ((0, 0, 1), (over[0], over[2])),
        ((0, 1, 0), (over[0], over[1], side[0], side[2])),
        ((0, 1, 1), (over[0],)),
    ):
        halo.append(to_block(jnp.stack(tiles), moved))
    state = attend_own(live, q, kv, 6, 2, state)
    done = {}
    for first, tiles in ((2, 6), (0, 2)):
        mixed, crossing = attend_halo(slab_at, live, q, state, halo, first, tiles)
        if not first:
            mixed, weight_c = lax.optimization_barrier((mixed, weight_c))
        crossed = across(crossing)
        for p in range(first // 2, (first + tiles) // 2):
            r = slice(2 * p - first, 2 * p - first + 2)
            done[p] = (mixed[r], crossed[r])
    weight_d = to_core(weight_c)
    for p in (3, 2, 1):
        moved = from_chip(jnp.concatenate(done[p]), p)
        done[p] = (moved[:2], moved[2:])
    same, cross = zip(*(done[p] for p in range(4)), strict=True)
    core = to_core(jnp.stack([piece[1] for piece in same + cross]))
    gate = branch_gate.reshape(1, -1)
    return output(slab_at, same, cross, core, out_weight, weight_c, weight_d, gate)[None]


def solution(mesh):
    in_specs = (
        P("slab", "heads", None),
        P(None, "heads"),
        P("heads", None),
        P(),
        P(),
        P(),
        P(),
        P(),
        P("slab", None),
    )
    out_specs = P("slab", "heads", None)
    return jax.shard_map(
        on_device,
        mesh=mesh,
        in_specs=in_specs,
        out_specs=out_specs,
        check_vma=False,
    )
```

```python
import jax
import jax.numpy as jnp
import numpy as np
from jax import lax
from jax.experimental import pallas as pl
from jax.experimental.pallas import tpu as pltpu
from jax.sharding import PartitionSpec as P


TILE = 384
HD = 128
MASK_ROWS = 16
NEG = -1e30

HALO = (
    ((0, 0, 1), (0, 2, 4, 6)),
    ((0, 1, 0), (0, 1, 4, 5)),
    ((1, 0, 0), (0, 1, 2, 3)),
    ((1, 0, 1), (0, 2)),
    ((1, 1, 0), (0, 1)),
    ((0, 1, 1), (0, 4)),
    ((1, 1, 1), (0,)),
)
OWN_AT = [((u >> 2) & 1, (u >> 1) & 1, u & 1) for u in range(8)]
HALO_AT = [
    tuple(-1 if moved[d] else ((u >> (2 - d)) & 1) for d in range(3)) for moved, us in HALO for u in us
]


def chip_of(s):
    return ((s >> 4) & 1) * 2 + ((s >> 2) & 1)


def corner_of(s):
    return ((s >> 3) & 1) * 2 + ((s >> 1) & 1)


def slot_of(s, core, p):
    return chip_of(s) ^ p ^ (core * corner_of(s))


def u_base(s):
    ut = ((s >> 4) ^ (s >> 5) ^ 1) & 1
    uh = ((s >> 2) ^ (s >> 3) ^ 1) & 1
    uw = (s ^ (s >> 1) ^ 1) & 1
    return ut * 4 + uh * 2 + uw


def chip_mask(p):
    return ((p >> 1) << 4) | ((p & 1) << 2)


def halo_mask(core, moved):
    mask = (moved[0] << 5) | (moved[1] << 3) | (moved[2] << 1)
    if core:
        mask |= (moved[1] << 4) | (moved[2] << 2)
    return mask


def busy(s):
    return slot_of(s, s & 1, 0) < 3


def to_chip(value, p):
    pairs = [(s, s ^ chip_mask(p)) for s in range(64) if busy(s ^ chip_mask(p))]
    return lax.ppermute(value, "slab", pairs)


def from_chip(value, p):
    pairs = [(s, s ^ chip_mask(p)) for s in range(64) if busy(s)]
    return lax.ppermute(value, "slab", pairs)


def across(value):
    pairs = [(64 * g + s, 64 * (1 - g) + s) for g in range(2) for s in range(64) if busy(s)]
    return lax.ppermute(value, ("heads", "slab"), pairs)


def weight_across(value):
    pairs = [(64 * g + s, 64 * (1 - g) + (s ^ 32)) for g in range(2) for s in range(64)]
    return lax.ppermute(value, ("heads", "slab"), pairs)


def to_core(value):
    return lax.ppermute(value, "slab", [(s, s ^ 1) for s in range(64)])


def to_block(value, moved):
    pairs = [(s, s ^ halo_mask(s & 1, moved)) for s in range(64) if busy(s)]
    return lax.ppermute(value, "slab", pairs)


def to_group(value):
    return lax.ppermute(value, "heads", [(0, 1), (1, 0)])


def whole(shape):
    return pl.BlockSpec(shape, lambda *_: (0,) * len(shape), pipeline_mode=pl.Buffered(1))


def modulate_kernel(x_ref, shift_ref, scale_ref, out_ref):
    rows = x_ref[0].astype(jnp.float32)
    centered = rows - jnp.mean(rows, axis=-1, keepdims=True)
    variance = jnp.mean(centered * centered, axis=-1, keepdims=True)
    out = centered * lax.rsqrt(variance + 1e-06) * (1.0 + scale_ref[...]) + shift_ref[...]
    out_ref[...] = out.astype(jnp.bfloat16)


def modulate(tokens, mod_shift, mod_scale):
    _, rows, width = tokens.shape
    step = 48
    return pl.pallas_call(
        modulate_kernel,
        out_shape=jax.ShapeDtypeStruct((rows, width), jnp.bfloat16),
        grid=(rows // step,),
        in_specs=[
            pl.BlockSpec((1, step, width), lambda i: (0, i, 0)),
            whole((1, width)),
            whole((1, width)),
        ],
        out_specs=pl.BlockSpec((step, width), lambda i: (i, 0)),
        compiler_params=pltpu.CompilerParams(vmem_limit_bytes=8 << 20),
        name="modulate",
    )(tokens, mod_shift.reshape(1, width), mod_scale.reshape(1, width))


def project_kernel(other, s_ref, x_ref, w_ref, qg_ref, kg_ref, mask_ref, out_ref):
    s = s_ref[0]
    rows = x_ref.shape[0]
    core = (s & 1) ^ other

    def normed(part, gain):
        part = part.astype(jnp.float32)
        return part * lax.rsqrt(jnp.mean(part * part, axis=-1, keepdims=True) + 1e-06) * gain

    def one_slot(i, _):
        slot = slot_of(s, core, i)

        @pl.when(slot < 3)
        def _():
            at = pl.multiple_of((core * 3 + slot) * (3 * HD), 3 * HD)
            acc = jnp.dot(
                x_ref[...], w_ref[:, pl.ds(at, 3 * HD)], preferred_element_type=jnp.float32
            ).astype(jnp.bfloat16)
            q = normed(acc[:, :HD], qg_ref[...]) * HD ** (-0.5)
            out_ref[i, :rows, :HD] = q.astype(jnp.bfloat16)
            out_ref[i, :rows, HD : 2 * HD] = normed(acc[:, HD : 2 * HD], kg_ref[...]).astype(
                jnp.bfloat16
            )
            out_ref[i, :rows, 2 * HD :] = acc[:, 2 * HD :]
            if out_ref.shape[1] > rows:
                out_ref[i, rows:, :] = mask_ref[...]

        @pl.when(slot >= 3)
        def _():
            out_ref[i] = jnp.zeros_like(out_ref[i])

        return 0

    lax.fori_loop(0, 4, one_slot, 0)


def project(slab_at, x, weight, query_gain, key_gain, mask_rows, other, with_mask):
    rows, _ = x.shape
    out_rows = rows + (MASK_ROWS if with_mask else 0)
    vmem = pl.BlockSpec(memory_space=pltpu.VMEM)
    return pl.pallas_call(
        lambda *refs: project_kernel(other, *refs),
        out_shape=jax.ShapeDtypeStruct((4, out_rows, 3 * HD), jnp.bfloat16),
        in_specs=[pl.BlockSpec(memory_space=pltpu.SMEM)] + [vmem] * 5,
        out_specs=vmem,
        compiler_params=pltpu.CompilerParams(vmem_limit_bytes=20 << 20),
    )(slab_at, x, weight, query_gain, key_gain, mask_rows)


def live_tables():
    table = np.full((8, 8, HD), HD, np.int32)
    for corner in range(8):
        signs = [((corner >> (2 - d)) & 1) * 2 - 1 for d in range(3)]
        for u in range(8):
            for k, at in enumerate(OWN_AT + HALO_AT):
                steps = [at[d] - ((u >> (2 - d)) & 1) for d in range(3)]
                if min(steps) >= -1:
                    table[corner, u, k] = 13 + sum(
                        w * g * t for w, g, t in zip((9, 3, 1), signs, steps, strict=True)
                    )
    return table


def block_of(s):
    return ((s >> 5) & 1) * 4 + corner_of(s)


def part_kernel(s_ref, w_ref, out_ref, sem):
    rows = out_ref.shape[0]
    start = pl.multiple_of((s_ref[0] & 1) * rows, rows)
    copy = pltpu.make_async_copy(w_ref.at[pl.ds(start, rows)], out_ref, sem)
    copy.start()
    copy.wait()


def weight_part(slab_at, weight):
    rows, width = weight.shape
    return pl.pallas_call(
        part_kernel,
        out_shape=jax.ShapeDtypeStruct((rows // 2, width), weight.dtype),
        grid_spec=pltpu.PrefetchScalarGridSpec(
            num_scalar_prefetch=1,
            grid=(1,),
            in_specs=[pl.BlockSpec(memory_space=pl.ANY)],
            out_specs=pl.BlockSpec(memory_space=pl.ANY),
            scratch_shapes=[pltpu.SemaphoreType.DMA(())],
        ),
        compiler_params=pltpu.CompilerParams(vmem_limit_bytes=1 << 20),
        name="weight_part",
    )(slab_at, weight)


def assemble_kernel(s_ref, *refs):
    base = u_base(s_ref[0])
    half = TILE // 2
    spot_ref, q_ref, kv_ref, live_ref = refs[10:14]
    entry = lax.broadcasted_iota(jnp.int32, (HD, HD), 0)
    lane = lax.broadcasted_iota(jnp.int32, (MASK_ROWS, HD), 1)
    for at, halves in enumerate((refs[:5], refs[5:10])):
        keep_ref, core_ref, *near = halves
        pieces = [(keep_ref, 0), (core_ref, 0)] + [(ref, dc) for ref in near for dc in range(2)]
        rows = slice(at * half, (at + 1) * half)
        for r, (ref, dc) in enumerate(pieces):
            u = base ^ r
            q_ref[u, rows] = ref[dc, :half, :HD]
            kv_ref[u, rows] = ref[dc, :half, HD:]
            if at == 0:
                marked = jnp.where(lane == 13, 1.0, ref[dc, half:, :HD].astype(jnp.float32))
                pick = jnp.where(entry == spot_ref[0, pl.ds(u, 1)], 1.0, 0.0)
                live = jnp.dot(
                    marked.astype(jnp.bfloat16),
                    pick.astype(jnp.bfloat16),
                    preferred_element_type=jnp.float32,
                )
                live_ref[pl.ds(u, 1)] = live[:1].astype(jnp.int32)
    for (_, us), send in zip(HALO, refs[14:]):
        for at, u in enumerate(us):
            send[at] = kv_ref[u]


def assemble(slab_at, halves):
    shapes = [
        ((8, TILE, HD), jnp.bfloat16),
        ((8, TILE, 2 * HD), jnp.bfloat16),
        ((8, HD), jnp.int32),
    ] + [((len(us), TILE, 2 * HD), jnp.bfloat16) for _, us in HALO[:3]]
    in_specs = []
    for keep, *_ in halves:
        rows = keep.shape[1]
        in_specs += [whole((1, rows, 3 * HD))] * 2 + [whole((2, rows, 3 * HD))] * 3
    in_specs.append(pl.BlockSpec((1, 8, HD), lambda i, s_ref: (block_of(s_ref[0]), 0, 0)))
    return pl.pallas_call(
        assemble_kernel,
        out_shape=[jax.ShapeDtypeStruct(*shape) for shape in shapes],
        grid_spec=pltpu.PrefetchScalarGridSpec(
            num_scalar_prefetch=1,
            grid=(1,),
            in_specs=in_specs,
            out_specs=[whole(shape) for shape, _ in shapes],
        ),
        compiler_params=pltpu.CompilerParams(vmem_limit_bytes=16 << 20),
        name="assemble",
    )(slab_at, *halves[0], *halves[1], jnp.asarray(live_tables()))


def fold(x, op):
    return op(op(x[:, :HD], x[:, HD : 2 * HD]), x[:, 2 * HD :])


def spread_max(x):
    return jnp.broadcast_to(jnp.max(x, axis=1, keepdims=True), x.shape)


def attend(u, first, count, live_ref, q, kv_ref, s_ref, list_ref, m_ref, l_ref, acc_ref, rescale):
    n = jnp.int32(0)
    for k in range(count):
        list_ref[n] = k
        n = n + live_ref[u, first + k]

    def score(base, group):
        def step(j, _):
            top = m_ref[...]
            for i in range(group):
                at = base + j * group + i
                scores = lax.dot_general(
                    q,
                    kv_ref[list_ref[at], :, :HD],
                    (((1,), (1,)), ((), ())),
                    preferred_element_type=jnp.float32,
                )
                s_ref[at] = scores
                top = jnp.maximum(top, fold(scores, jnp.maximum))
            m_ref[...] = top
            return 0

        return step

    def weigh(base, group):
        def step(j, _):
            top = m_ref[...]
            top = jnp.concatenate([top, top, top], axis=1)
            total = l_ref[...]
            acc = acc_ref[...]
            for i in range(group):
                at = base + j * group + i
                raised = jnp.exp(s_ref[at] - top)
                total = total + fold(raised, jnp.add)
                acc = acc + jnp.dot(
                    raised.astype(jnp.bfloat16),
                    kv_ref[list_ref[at], :, HD:],
                    preferred_element_type=jnp.float32,
                )
            l_ref[...] = total
            acc_ref[...] = acc
            return 0

        return step

    def each(make):
        lax.fori_loop(0, n >> 2, make(0, 4), 0)
        lax.fori_loop(0, (n >> 1) & 1, make((n >> 2) << 2, 2), 0)
        lax.fori_loop(0, n & 1, make((n >> 1) << 1, 1), 0)

    each(score)
    rescale(spread_max(m_ref[...]))
    each(weigh)


def own_kernel(first, live_ref, q_ref, kv_ref, *refs):
    u = first + pl.program_id(0)
    m_ref, l_ref, acc_ref, s_ref, list_ref = refs[-5:]
    m, l, acc = m_ref.at[0], l_ref.at[0], acc_ref.at[0]
    m[...] = jnp.full_like(m[...], NEG)

    def rescale(top):
        m[...] = top
        l[...] = jnp.zeros_like(l[...])
        acc[...] = jnp.zeros_like(acc[...])

    attend(u, 0, 8, live_ref, q_ref[0], kv_ref, s_ref, list_ref, m, l, acc, rescale)


def attend_own(live, q, kv, first, tiles, prior):
    per_u = pl.BlockSpec((1, TILE, HD), lambda u, *_: (first + u, 0, 0))
    state = jax.ShapeDtypeStruct((8, TILE, HD), jnp.float32)
    return pl.pallas_call(
        lambda *refs: own_kernel(first, *refs),
        out_shape=[state, state, state],
        grid_spec=pltpu.PrefetchScalarGridSpec(
            num_scalar_prefetch=1,
            grid=(tiles,),
            in_specs=[per_u, whole((8, TILE, 2 * HD))]
            + [pl.BlockSpec(memory_space=pl.ANY)] * len(prior),
            out_specs=[per_u] * 3,
            scratch_shapes=[pltpu.VMEM((8, TILE, TILE), jnp.float32), pltpu.SMEM((9,), jnp.int32)],
        ),
        input_output_aliases={3 + i: i for i in range(len(prior))},
        compiler_params=pltpu.CompilerParams(vmem_limit_bytes=14 << 20),
    )(live, q, kv, *prior)


def halo_kernel(first, s_ref, live_ref, q_ref, m_in, l_in, acc_in, *refs):
    pieces, (near_ref, far_ref, kv_ref, score_ref, m_ref, l_ref, acc_ref, list_ref, sems) = refs[:6], refs[6:]

    @pl.when(pl.program_id(0) == 0)
    def _():
        at = 0
        copies = []
        for i, piece in enumerate(pieces):
            to = kv_ref.at[pl.ds(at, piece.shape[0])]
            copies.append(pltpu.make_async_copy(piece, to, sems.at[i]))
            at += piece.shape[0]
        for copy in copies:
            copy.start()
        for copy in copies:
            copy.wait()

    u = (first + pl.program_id(0)) ^ u_base(s_ref[0])
    m_ref[...] = m_in[0]

    def rescale(top):
        m_ref[...] = top
        shrink = jnp.exp(m_in[0] - top)
        l_ref[...] = l_in[0] * shrink
        acc_ref[...] = acc_in[0] * shrink

    count = len(HALO_AT)
    attend(u, 8, count, live_ref, q_ref[0], kv_ref, score_ref, list_ref, m_ref, l_ref, acc_ref, rescale)
    total = jnp.sum(l_ref[...], axis=1, keepdims=True)
    mixed = (acc_ref[...] / total).astype(jnp.bfloat16)
    near_ref[0] = mixed[: TILE // 2]
    far_ref[0] = mixed[TILE // 2 :]


def attend_halo(slab_at, live, q, state, pieces, first, tiles):
    per_u = pl.BlockSpec((1, TILE, HD), lambda r, s_ref, *_: ((first + r) ^ u_base(s_ref[0]), 0, 0))
    count = len(HALO_AT)
    return pl.pallas_call(
        lambda *refs: halo_kernel(first, *refs),
        out_shape=[jax.ShapeDtypeStruct((tiles, TILE // 2, HD), jnp.bfloat16)] * 2,
        grid_spec=pltpu.PrefetchScalarGridSpec(
            num_scalar_prefetch=2,
            grid=(tiles,),
            in_specs=[per_u] * 4 + [pl.BlockSpec(memory_space=pl.ANY)] * len(pieces),
            out_specs=[pl.BlockSpec((1, TILE // 2, HD), lambda r, *_: (r, 0, 0))] * 2,
            scratch_shapes=[
                pltpu.VMEM((count, TILE, 2 * HD), jnp.bfloat16),
                pltpu.VMEM((count, TILE, TILE), jnp.float32),
            ]
            + [pltpu.VMEM((TILE, HD), jnp.float32)] * 3
            + [pltpu.SMEM((count + 1,), jnp.int32), pltpu.SemaphoreType.DMA((len(pieces),))],
        ),
        compiler_params=pltpu.CompilerParams(vmem_limit_bytes=24 << 20),
    )(slab_at, live, q, *state, *pieces)


def output_kernel(s_ref, *refs):
    same, cross, (core_ref, w_ref, wc_ref, wd_ref, gate_ref, out_ref, x_ref, xc_ref, xd_ref) = (
        refs[:4],
        refs[4:8],
        refs[8:],
    )
    s = s_ref[0]
    mine = s & 1

    for p in range(4):
        for core, pieces in (
            (mine, (same[p].at[0], cross[p].at[0])),
            (1 - mine, (core_ref.at[p], core_ref.at[4 + p])),
        ):
            slot = slot_of(s, core, p)
            far_ref = xc_ref if core is mine else xd_ref

            @pl.when(slot < 3)
            def _(core=core, slot=slot, pieces=pieces, far_ref=far_ref):
                x_ref[:, pl.ds(pl.multiple_of((core * 3 + slot) * HD, HD), HD)] = pieces[0][...]
                far_ref[:, pl.ds(pl.multiple_of(slot * HD, HD), HD)] = pieces[1][...]

    cols = 1024

    def one_part(n, _):
        at = pl.ds(pl.multiple_of(n * cols, cols), cols)

        def dot(x, w):
            return jnp.dot(x[...], w[:, at], preferred_element_type=jnp.float32)

        near = dot(x_ref, w_ref).astype(jnp.bfloat16).astype(jnp.float32)
        far = (dot(xc_ref, wc_ref) + dot(xd_ref, wd_ref)).astype(jnp.bfloat16).astype(jnp.float32)
        out_ref[:, at] = (gate_ref[:, at] * (near + far)).astype(jnp.bfloat16)
        return 0

    lax.fori_loop(0, out_ref.shape[1] // cols, one_part, 0)


def output(slab_at, same, cross, core, weight, weight_c, weight_d, gate):
    inner, width = weight.shape
    half = TILE // 2
    vmem = pl.BlockSpec(memory_space=pltpu.VMEM)
    return pl.pallas_call(
        output_kernel,
        out_shape=jax.ShapeDtypeStruct((half, width), jnp.bfloat16),
        in_specs=[pl.BlockSpec(memory_space=pltpu.SMEM)] + [vmem] * 13,
        out_specs=vmem,
        scratch_shapes=[
            pltpu.VMEM((half, inner), jnp.bfloat16),
            pltpu.VMEM((half, inner // 2), jnp.bfloat16),
            pltpu.VMEM((half, inner // 2), jnp.bfloat16),
        ],
        compiler_params=pltpu.CompilerParams(vmem_limit_bytes=20 << 20),
        name="output",
    )(slab_at, *same, *cross, core, weight, weight_c, weight_d, gate)


def on_device(
    tokens,
    qkv_weight,
    out_weight,
    query_gain,
    key_gain,
    mod_shift,
    mod_scale,
    branch_gate,
    block_mask,
):
    slab_at = lax.axis_index("slab").astype(jnp.int32).reshape(1)
    own = modulate(tokens, mod_shift, mod_scale)
    far = to_group(own)
    mask_rows = jnp.pad(
        jnp.broadcast_to(block_mask.astype(jnp.bfloat16), (MASK_ROWS, 27)), ((0, 0), (0, 3 * HD - 27))
    )
    gains = (query_gain.reshape(1, HD), key_gain.reshape(1, HD))
    part = weight_part(slab_at, out_weight)
    halves = []
    x = own
    for at in range(2):
        send = project(slab_at, x, qkv_weight, *gains, mask_rows, 1, at == 0)
        if at:
            send, part = lax.optimization_barrier((send, part))
        core = to_core(send)
        keep = project(slab_at, x, qkv_weight, *gains, mask_rows, 0, at == 0)
        near = []
        for p in (1, 2, 3):
            near.append(to_chip(jnp.stack([keep[p], core[p]]), p))
        x = far
        halves.append((keep, core, *near))
    weight_c = weight_across(part)
    q, kv, live, *sends = assemble(slab_at, halves)
    halo = []
    for piece, (moved, _) in zip(sends, HALO):
        halo.append(to_block(piece, moved))
    state = attend_own(live, q, kv, 0, 6, ())
    *state, side, over = lax.optimization_barrier((*state, halo[0], halo[2]))
    halo = [side, halo[1], over]
    for moved, tiles in (
        ((0, 0, 1), (over[0], over[2])),
        ((0, 1, 0), (over[0], over[1], side[0], side[2])),
        ((0, 1, 1), (over[0],)),
    ):
        halo.append(to_block(jnp.stack(tiles), moved))
    state = attend_own(live, q, kv, 6, 2, state)
    done = {}
    for first, tiles in ((2, 6), (0, 2)):
        mixed, crossing = attend_halo(slab_at, live, q, state, halo, first, tiles)
        if not first:
            mixed, weight_c = lax.optimization_barrier((mixed, weight_c))
        crossed = across(crossing)
        for p in range(first // 2, (first + tiles) // 2):
            r = slice(2 * p - first, 2 * p - first + 2)
            done[p] = (mixed[r], crossed[r])
    weight_d = to_core(weight_c)
    for p in (3, 2, 1):
        moved = from_chip(jnp.concatenate(done[p]), p)
        done[p] = (moved[:2], moved[2:])
    same, cross = zip(*(done[p] for p in range(4)), strict=True)
    core = to_core(jnp.stack([piece[1] for piece in same + cross]))
    gate = branch_gate.reshape(1, -1)
    return output(slab_at, same, cross, core, out_weight, weight_c, weight_d, gate)[None]


def solution(mesh):
    in_specs = (
        P("slab", "heads", None),
        P(None, "heads"),
        P("heads", None),
        P(),
        P(),
        P(),
        P(),
        P(),
        P("slab", None),
    )
    out_specs = P("slab", "heads", None)
    return jax.shard_map(
        on_device,
        mesh=mesh,
        in_specs=in_specs,
        out_specs=out_specs,
        check_vma=False,
    )
```
